256 devices in a mesh: dom: 8 (over z), cls: 32 (over x, y, core).
Axes of the slice: x: 4, y: 4, z: 8, core: 2. Of those that a mesh axis runs over, the one named last changes fastest.
Arguments:
- images: bfloat16 [8192, 64, 256], P(('dom', 'cls'))
- references: bfloat16 [512, 64, 256], P('cls')
- ctf_table: float32 [64, 64], replicated, may hold values from 0.2 to 1
- defocus: int32 [8192], P(('dom', 'cls')), may hold values from 0 to 63
- priors: int32 [8192, 8], P(('dom', 'cls')), may hold values from 0 to 511, as said below
Outputs:
- new_refs: float32 [512, 64, 256], P('cls', 'dom')
The draws below stay inside these ranges and needn't reach their ends.
Inputs may be any that keep to these rules, and one draw needn't show every extreme that they name: `priors`: the owner of class k is index k // 16 of cls. Among the prior entries of one device's particles at most 10 name classes of any one owner; in each index of dom one owner is named exactly 10 times by every device.
All inputs are finite; a program needn't handle non-finite values.
Results may differ from the reference program's by a relative error of at most 0.011.
Values may be sent and summed in bfloat16 or wider, within the bound.
No kernel may reach another device: no remote copies, remote signals or barrier semaphores. Data moves between devices by JAX's collectives and lax.ppermute only.
A program may use at most 128 MiB of HBM per device.

```python
import math
import jax
import jax.numpy as jnp
from jax import lax

CYCLES = 64
ANGLES = 256
HARM = 128
PRIOR = 8
CLS_DEV = 16
CLASSES = 512
GROUPS = 64
NP_DEV = 32
PARTICLES = 8192
CAP = 10
N_DOM = 8
N_CLS = 32


def prior_table(key):
    blocks = N_DOM * N_CLS
    per_block = NP_DEV * PRIOR
    seats = N_CLS * CAP
    hot_owner = jax.random.randint(jax.random.fold_in(key, 101), (N_DOM,), 0, N_CLS)
    hot_block = jnp.repeat(hot_owner, N_CLS)
    block_keys = jax.random.split(jax.random.fold_in(key, 102), blocks)

    def one_block(block_key, hottest):
        key_seat, key_order, key_class = jax.random.split(block_key, 3)
        others = jax.random.permutation(key_seat, seats - CAP).astype(jnp.int32)
        chosen = jnp.concatenate([jnp.arange(CAP, dtype=jnp.int32), CAP + others[:per_block - CAP]])
        owner = (chosen // CAP + hottest) % N_CLS
        owner = jax.random.permutation(key_order, owner)
        within = jax.random.randint(key_class, (per_block,), 0, CLS_DEV)
        return owner * CLS_DEV + within
    return jax.vmap(one_block)(block_keys, hot_block).reshape(PARTICLES, PRIOR).astype(jnp.int32)


def reference_table(key):
    spread = 4.7 / math.sqrt(CYCLES * ANGLES)
    return spread * jax.random.normal(jax.random.fold_in(key, 201), (CLASSES, CYCLES, ANGLES), jnp.float32)


def draw_priors(key, part):
    return prior_table(key)


def draw_references(key, part):
    table = reference_table(key)
    return table.astype(jnp.bfloat16)


def draw_images(key, part):
    image = jax.random.normal(jax.random.fold_in(key, 302), (PARTICLES, CYCLES, ANGLES), jnp.float32)
    return image.astype(jnp.bfloat16)


def set_ends(entries, rng, smallest, high):
    extent = entries.shape
    index_at = [jax.random.randint(jax.random.fold_in(rng, axis), (), 0, extent[axis]) for axis in range(len(extent))]
    entries = entries.at[tuple(index_at)].set(smallest)
    longest = extent.index(max(extent))
    index_at[longest] = (index_at[longest] + 1) % extent[longest]
    return entries.at[tuple(index_at)].set(high)


def setup_inputs(seed: int = 0) -> dict:
    splits = jax.random.split(jax.random.key(seed), 6)
    images = draw_images(jax.random.fold_in(splits[5], 71), 0)
    references = draw_references(jax.random.fold_in(splits[5], 71), 0)
    ctf_table = jnp.clip(jax.random.uniform(splits[2], (GROUPS, CYCLES), jnp.float32, 0.2, 1.0), 0.2, 1.0)
    defocus = set_ends(jax.random.randint(splits[3], (PARTICLES,), 0, GROUPS), jax.random.fold_in(splits[3], 1), 0, GROUPS - 1).astype(jnp.int32)
    priors = draw_priors(jax.random.fold_in(splits[5], 71), 0)
    return dict(images=images, references=references, ctf_table=ctf_table, defocus=defocus, priors=priors)


def angle_tables(angles):
    harm_count = angles // 2
    angle_index = jnp.arange(angles, dtype=jnp.int32)
    harm_index = jnp.arange(harm_count, dtype=jnp.int32)
    phase_grid = (angle_index[:, None] * harm_index[None, :]) % angles
    angle_grid = (2.0 * jnp.pi / angles) * phase_grid.astype(jnp.float32)
    cosine = jnp.cos(angle_grid)
    sine_grid = jnp.sin(angle_grid)
    forward = jnp.concatenate([cosine, sine_grid], axis=1)
    harm_weight = jnp.where(harm_index == 0, 1.0, 2.0).astype(jnp.float32) / angles
    inverse = jnp.concatenate([cosine.T * harm_weight[:, None], -sine_grid.T * harm_weight[:, None]], axis=0)
    return forward, inverse


def to_harmonics(frames, forward):
    frame_count, cycle_count, angles = frames.shape
    flat_rows = jnp.dot(frames.reshape(frame_count * cycle_count, angles), forward.astype(jnp.bfloat16), preferred_element_type=jnp.float32)
    return flat_rows.astype(jnp.bfloat16).reshape(frame_count, cycle_count, forward.shape[1])


def slot_scores(part_block, ref_block, ctf_block, inverse):
    harm_count = part_block.shape[2] // 2
    part_cos = part_block[:, :, :harm_count].astype(jnp.float32)
    part_sin = part_block[:, :, harm_count:].astype(jnp.float32)
    ref_cos = ref_block[:, :, :harm_count].astype(jnp.float32)
    ref_sin = ref_block[:, :, harm_count:].astype(jnp.float32)
    ctf_weight = ctf_block[:, :, None]
    real_part = jnp.sum(ctf_weight * (part_cos * ref_cos + part_sin * ref_sin), axis=1)
    imag_part = jnp.sum(ctf_weight * (part_cos * ref_sin - part_sin * ref_cos), axis=1)
    joined = jnp.concatenate([real_part, imag_part], axis=1)
    return jnp.dot(joined, inverse, precision=lax.Precision.HIGHEST)


def accumulate_terms(part_block, weights, ctf_block, forward):
    harm_count = part_block.shape[2] // 2
    spectrum = jnp.dot(weights, forward, precision=lax.Precision.HIGHEST)
    w_cos = spectrum[:, None, :harm_count]
    w_sin = spectrum[:, None, harm_count:]
    part_cos = part_block[:, :, :harm_count].astype(jnp.float32)
    part_sin = part_block[:, :, harm_count:].astype(jnp.float32)
    ctf_weight = ctf_block[:, :, None]
    real_part = ctf_weight * (part_cos * w_cos + part_sin * w_sin)
    imag_part = ctf_weight * (part_sin * w_cos - part_cos * w_sin)
    term_rows = jnp.concatenate([real_part, imag_part], axis=2)
    norm_rows = ctf_block * ctf_block * jnp.sum(weights, axis=1)[:, None]
    return term_rows, norm_rows


def reference(images, references, ctf_table, defocus, priors):
    forward, inverse = angle_tables(ANGLES)
    ref_harm = to_harmonics(references, forward)
    block_size = 64
    block_count = PARTICLES // block_size
    image_blocks = images.reshape(block_count, block_size, CYCLES, ANGLES)
    group_blocks = defocus.reshape(block_count, block_size)
    prior_blocks = priors.reshape(block_count, block_size, PRIOR)

    def scan_step(carry, inputs):
        class_sums, class_norms = carry
        frames, groups, classes = inputs
        harmonic = to_harmonics(frames, forward)
        part_block = jnp.repeat(harmonic, PRIOR, axis=0)
        flat_class = classes.reshape(-1).astype(jnp.int32)
        ref_block = ref_harm[flat_class]
        ctf_block = jnp.repeat(ctf_table[groups], PRIOR, axis=0)
        scores = slot_scores(part_block, ref_block, ctf_block, inverse)
        grouped = scores.reshape(block_size, PRIOR * ANGLES)
        highest = jnp.max(grouped, axis=1, keepdims=True)
        log_total = highest + jnp.log(jnp.sum(jnp.exp(grouped - highest), axis=1, keepdims=True))
        weights = jnp.exp(grouped - log_total).reshape(block_size * PRIOR, ANGLES)
        term_rows, norm_rows = accumulate_terms(part_block, weights, ctf_block, forward)
        return (class_sums.at[flat_class].add(term_rows), class_norms.at[flat_class].add(norm_rows)), None

    initial = (jnp.zeros((CLASSES, CYCLES, 2 * HARM), jnp.float32), jnp.zeros((CLASSES, CYCLES), jnp.float32))
    (class_sums, class_norms), ignored = lax.scan(scan_step, initial, (image_blocks, group_blocks, prior_blocks))
    return class_sums / (class_norms + 1.0)[:, :, None]
```

```python
import numpy as np

import jax
import jax.numpy as jnp
from jax import lax
from jax.experimental import pallas as pl
from jax.experimental.pallas import tpu as pltpu
from jax.sharding import PartitionSpec as P

F32 = jnp.float32
BF16 = jnp.bfloat16
NT = (((1,), (1,)), ((), ()))
LANES = 128


def tables(angles, slices):
    harm = angles // 2
    per = harm // slices
    s, c, m = np.meshgrid(np.arange(slices), np.arange(2), np.arange(per), indexing="ij")
    harmonic = (s * per + m).reshape(-1)
    is_sin = c.reshape(-1)
    phase = (harmonic[:, None] * np.arange(angles)[None, :]) % angles
    grid = phase * (2.0 * np.pi / angles)
    cosine = np.cos(grid).astype(np.float32)
    sine = np.sin(grid).astype(np.float32)
    forward = np.where(is_sin[:, None] == 0, cosine, sine).astype(np.float32)
    weight = np.where(harmonic == 0, 1.0, 2.0).astype(np.float32) / angles
    inverse = (np.where(is_sin[:, None] == 0, cosine, -sine) * weight[:, None]).T.astype(np.float32)
    column = is_sin * harm + harmonic
    order = np.zeros((angles, angles), np.float32)
    order[np.arange(angles), column] = 1.0
    return forward, inverse, order


def lane_swap(arrays):
    n = len(arrays)
    width = LANES // n
    arrays = list(arrays)
    lane = lax.broadcasted_iota(jnp.int32, arrays[0].shape, 1)
    step = n // 2
    while step >= 1:
        shift = width * step
        low = (lane & shift) == 0
        for a in range(n):
            if a & step == 0:
                x, y = arrays[a], arrays[a + step]
                arrays[a] = jnp.where(low, x, pltpu.roll(y, shift, 1))
                arrays[a + step] = jnp.where(low, pltpu.roll(x, LANES - shift, 1), y)
        step //= 2
    return arrays


def harmonics_kernel(img_ref, ref_ref, pri_ref, def_ref, fwd_ref, out_ref, img_s, ref_s, int_s):
    n, cyc, ang = img_ref.shape
    own = ref_ref.shape[0]
    dest = out_ref.shape[0]
    for k in range(ang // LANES):
        lanes = slice(k * LANES, (k + 1) * LANES)
        img_s[k] = img_ref[:, :, lanes].astype(F32).reshape(n * cyc, LANES)
        ref_s[k] = ref_ref[:, :, lanes].astype(F32).reshape(own * cyc, LANES)
    half = cyc // 2
    fwd = fwd_ref[...]

    def part(src, count, column):
        group = LANES // count
        for c in range(half // group):
            block = jnp.concatenate(
                [
                    jnp.concatenate(
                        [
                            src[k, pl.ds(2 * (group * c + q) + odd, count, stride=cyc), :]
                            for odd in range(2)
                            for q in range(group)
                        ],
                        axis=0,
                    )
                    for k in range(ang // LANES)
                ],
                axis=1,
            ).astype(BF16)
            y = lax.dot_general(fwd, block, NT, preferred_element_type=F32)
            y = y.reshape(dest, 8, 2 * LANES)
            y = jnp.concatenate([y[:, :, :LANES], y[:, :, LANES:]], axis=1)
            out_ref[:, :, column + c * LANES : column + (c + 1) * LANES] = y.astype(BF16)

    part(img_s, n, 0)
    part(ref_s, own, half * n)
    pri = pri_ref[...]
    eye = (
        lax.broadcasted_iota(jnp.int32, (8, 8), 0) == lax.broadcasted_iota(jnp.int32, (8, 8), 1)
    ).astype(F32)
    owner = (pri // own).astype(F32)
    within = (pri - (pri // own) * own).astype(F32)
    int_s[...] = jnp.zeros_like(int_s)
    int_s[0:8, 0:n] = lax.dot_general(eye, owner, NT, preferred_element_type=F32)
    int_s[8:16, 0:n] = lax.dot_general(eye, within, NT, preferred_element_type=F32)
    int_s[0:1, n : 2 * n] = def_ref[...].astype(F32)
    column = half * (n + own)
    out_ref[:, :, column : column + LANES] = jnp.broadcast_to(
        int_s[...].astype(BF16)[None], (dest, 16, LANES)
    )


def one_hot(row, count):
    index = lax.broadcasted_iota(jnp.int32, (count, row.shape[1]), 0)
    return jnp.where(index == row, 1.0, 0.0).astype(BF16)


def flip_rows(x):
    return pltpu.roll(x, 4, x.ndim - 2)


def score_kernel(own, in_ref, ctf_ref, x_ref, cp_ref, cid_ref, c_ref, cq_s, rt_s, x_s):
    src = in_ref.shape[0]
    groups, cyc = ctf_ref.shape
    half = cyc // 2
    total = cp_ref.shape[1]
    n = total // src
    classes = rt_s.shape[1]
    col_r = half * n
    col_i = half * (n + own)
    per = LANES // n
    per_r = LANES // own
    blocks = src // per

    ctf_t = ctf_ref[...].T
    for b in range(blocks):
        lanes = slice(b * LANES, (b + 1) * LANES)
        v = lane_swap(
            [in_ref[per * b + i, :, col_i : col_i + LANES].astype(F32) for i in range(per)]
        )
        cid_ref[:, lanes] = (v[0][0:8] * float(own) + v[0][8:16]).astype(jnp.int32)
        group = v[1][0:1].astype(jnp.int32)
        hot = (lax.broadcasted_iota(jnp.int32, (groups, LANES), 0) == group).astype(F32)
        c_ref[:, lanes] = jnp.dot(
            ctf_t, hot, precision=lax.Precision.HIGHEST, preferred_element_type=F32
        )

    def unpack_r(c, carry):
        col = pl.multiple_of(col_r + c * LANES, LANES)
        for b in range(src // per_r):
            v = lane_swap(
                [in_ref[per_r * b + i, :, pl.ds(col, LANES)].astype(F32) for i in range(per_r)]
            )
            for q in range(per_r):
                row = pl.multiple_of((per_r * c + q) * 16, 16)
                rt_s[pl.ds(row, 16), b * LANES : (b + 1) * LANES] = v[q].astype(BF16)
        return carry

    lax.fori_loop(0, half // per_r, unpack_r, 0)

    upper = lax.broadcasted_iota(jnp.int32, (16, LANES), 0) % 8 >= 4

    def unpack_p(c, carry):
        col = pl.multiple_of(c * LANES, LANES)
        for b in range(blocks):
            lanes = slice(b * LANES, (b + 1) * LANES)
            v = lane_swap(
                [in_ref[per * b + i, :, pl.ds(col, LANES)].astype(F32) for i in range(per)]
            )
            ctf = c_ref[pl.ds(pl.multiple_of(c * 2 * per, 2 * per), 2 * per), lanes]
            for q in range(per):
                row = pl.multiple_of((per * c + q) * 16, 16)
                scale = jnp.concatenate(
                    [
                        jnp.broadcast_to(ctf[2 * q + odd : 2 * q + odd + 1], (8, LANES))
                        for odd in range(2)
                    ],
                    axis=0,
                )
                p = v[q] * scale
                cp_ref[pl.ds(row, 16), lanes] = p
                swapped = flip_rows(p.reshape(2, 8, LANES)).reshape(16, LANES)
                cq_s[pl.ds(row, 16), lanes] = jnp.where(upper, swapped, -swapped)
        return carry

    lax.fori_loop(0, half // per, unpack_p, 0)

    wide = 256
    low = lax.broadcasted_iota(jnp.int32, (8, wide), 0) < 4

    def chunk(t, carry):
        col = pl.multiple_of(t * wide, wide)
        cols = pl.ds(col, wide)
        for j in range(8):
            hot = one_hot(cid_ref[j : j + 1, cols], classes)
            picked = jnp.dot(rt_s[...], hot, preferred_element_type=F32)
            re = jnp.sum((cp_ref[:, cols] * picked).reshape(cyc, 8, wide), axis=0)
            im = jnp.sum((cq_s[:, cols] * picked).reshape(cyc, 8, wide), axis=0)
            x_s[j, :, cols] = jnp.where(low, re + flip_rows(re), im + flip_rows(im))
        return carry

    lax.fori_loop(0, total // wide, chunk, 0)

    for b in range(blocks):
        lanes = slice(b * LANES, (b + 1) * LANES)
        for u in range(8 // per):
            v = lane_swap([x_s[per * u + j, :, lanes] for j in range(per)])
            for i in range(per):
                x_ref[per * b + i, :, u * LANES : (u + 1) * LANES] = v[i]


def weight_kernel(x_ref, inv_ref, fwd_ref, out_ref):
    src, rows, slots = x_ref.shape
    ang = inv_ref.shape[0]
    high = lax.Precision.HIGHEST
    x = x_ref[...].reshape(src * rows, slots)
    score = jnp.dot(inv_ref[...], x, precision=high, preferred_element_type=F32)

    def over_slots(row, op):
        row = op(row[:, :LANES], row[:, LANES:])
        row = op(row, pltpu.roll(row, 64, 1))
        row = op(row, pltpu.roll(row, 32, 1))
        return jnp.concatenate([row, row], axis=1)

    top = jnp.broadcast_to(jnp.max(score, axis=0, keepdims=True), (8, slots))
    top = over_slots(top, jnp.maximum)[0:1]
    grown = jnp.exp(score - top)
    mass = jnp.broadcast_to(jnp.sum(grown, axis=0, keepdims=True), (8, slots))
    mass = over_slots(mass, jnp.add)[0:1]
    weight = grown * (1.0 / mass)
    spectrum = jnp.dot(fwd_ref[...], weight, precision=high, preferred_element_type=F32)
    out_ref[...] = spectrum.reshape(src, rows, slots)


def sum_kernel(w_ref, cp_ref, cid_ref, c_ref, out_ref, w_s, t_s, sum_s):
    src = w_ref.shape[0]
    feats, total = cp_ref.shape
    cyc = c_ref.shape[0]
    classes = out_ref.shape[2]
    doms = out_ref.shape[0]
    n = total // src
    per = LANES // n
    for b in range(src // per):
        lanes = slice(b * LANES, (b + 1) * LANES)
        for u in range(8 // per):
            v = lane_swap(
                [w_ref[per * b + i, :, u * LANES : (u + 1) * LANES] for i in range(per)]
            )
            for j in range(per):
                w_s[per * u + j, :, lanes] = v[j]

    wide = 512
    low = lax.broadcasted_iota(jnp.int32, (8, wide), 0) < 4
    sum_s[...] = jnp.zeros_like(sum_s)

    def step(s, carry):
        j = s // (total // wide)
        col = pl.multiple_of((s % (total // wide)) * wide, wide)
        cols = pl.ds(col, wide)
        w = w_s[j, :, cols]
        turned = flip_rows(w)
        wc = jnp.where(low, w, turned)
        ws = jnp.where(low, turned, -w)
        p = cp_ref[:, cols].reshape(cyc, 8, wide)
        term = p * wc[None] + flip_rows(p) * ws[None]
        c = c_ref[:, cols]
        t_s[0:feats] = term.reshape(feats, wide).astype(BF16)
        t_s[feats : feats + cyc] = (c * c * w[0:1]).astype(BF16)
        hot = one_hot(cid_ref[pl.ds(j, 1), cols], classes)
        sum_s[...] += lax.dot_general(t_s[...], hot, NT, preferred_element_type=F32)
        return carry

    lax.fori_loop(0, 8 * (total // wide), step, 0)
    rows = feats // doms
    part = cyc // doms
    for d in range(doms):
        out_ref[d, 0:rows] = sum_s[d * rows : (d + 1) * rows].astype(BF16)
        out_ref[d, rows : rows + part] = sum_s[
            feats + d * part : feats + (d + 1) * part
        ].astype(BF16)


def regroup_kernel(in_ref, out_ref, s_s):
    doms, rows, classes = in_ref.shape
    s_s[...] = jnp.sum(in_ref[...].astype(F32), axis=0)
    owners = out_ref.shape[0]
    own = classes // owners
    per = LANES // own
    for b in range(classes // LANES):
        lanes = slice(b * LANES, (b + 1) * LANES)
        sums = lane_swap([s_s[8 * q : 8 * q + 8, lanes] for q in range(per)])
        norm = s_s[8 * per : 8 * per + 8, lanes]
        norms = lane_swap([jnp.broadcast_to(norm[q : q + 1], (8, LANES)) for q in range(per)])
        for k in range(per):
            out_ref[per * b + k] = jnp.concatenate([sums[k], norms[k]], axis=0).astype(BF16)


def finish_kernel(in_ref, order_ref, out_ref):
    src = in_ref.shape[0]
    own, part, width = out_ref.shape
    both = in_ref[...].astype(F32)
    x = jnp.concatenate([both[:, 0:8].reshape(src * 8, LANES), both[0, 8:16]], axis=0).astype(BF16)
    a = lax.broadcasted_iota(jnp.int32, (LANES, LANES), 0)
    b = lax.broadcasted_iota(jnp.int32, (LANES, LANES), 1)
    turn = jnp.where((a % own) * part + a // own == b, 1.0, 0.0).astype(BF16)
    x = jnp.dot(x, turn, preferred_element_type=F32)
    sums = x[0 : src * 8].T.astype(BF16)
    sums = jnp.dot(sums, order_ref[...], preferred_element_type=F32)
    norm = x[src * 8 :].T[:, 0:1]
    out_ref[...] = (sums / (norm + 1.0)).reshape(own, part, width)


def call(kernel, shapes, scratch, *args):
    many = isinstance(shapes, (list, tuple)) and not hasattr(shapes, "dtype")
    spec = pl.BlockSpec(memory_space=pltpu.VMEM)
    return pl.pallas_call(
        kernel,
        out_shape=shapes,
        in_specs=[spec] * len(args),
        out_specs=[spec] * len(shapes) if many else spec,
        scratch_shapes=scratch,
        compiler_params=pltpu.CompilerParams(vmem_limit_bytes=48 << 20),
    )(*args)


def on_device(images, references, ctf_table, defocus, priors):
    owners = lax.axis_size("cls")
    doms = lax.axis_size("dom")
    n, cyc, ang = images.shape
    own = references.shape[0]
    total = owners * n
    classes = owners * own
    feats = 8 * cyc
    forward, inverse, order = tables(ang, owners)
    shape = jax.ShapeDtypeStruct

    def exchange(x, axis):
        return lax.all_to_all(x, axis, split_axis=0, concat_axis=0, tiled=True)

    width = (cyc // 2) * (n + own) + LANES
    sent = call(
        harmonics_kernel,
        shape((owners, 16, width), BF16),
        [
            pltpu.VMEM((ang // LANES, n * cyc, LANES), F32),
            pltpu.VMEM((ang // LANES, own * cyc, LANES), F32),
            pltpu.VMEM((16, LANES), F32),
        ],
        images,
        references,
        priors,
        defocus.reshape(1, n),
        jnp.asarray(forward, BF16),
    )
    got = exchange(sent, "cls")
    x, cp, cid, ctf = call(
        lambda *refs: score_kernel(own, *refs),
        [
            shape((owners, 8, 8 * n), F32),
            shape((feats, total), F32),
            shape((8, total), jnp.int32),
            shape((cyc, total), F32),
        ],
        [
            pltpu.VMEM((feats, total), F32),
            pltpu.VMEM((feats, classes), BF16),
            pltpu.VMEM((8, 8, total), F32),
        ],
        got,
        ctf_table,
    )
    x = exchange(x, "cls")
    spectrum = call(
        weight_kernel,
        shape((owners, 8, 8 * n), F32),
        [],
        x,
        jnp.asarray(inverse),
        jnp.asarray(forward),
    )
    spectrum = exchange(spectrum, "cls")
    sums = call(
        sum_kernel,
        shape((doms, feats // doms + cyc // doms, classes), BF16),
        [
            pltpu.VMEM((8, 8, total), F32),
            pltpu.VMEM((feats + cyc, 512), BF16),
            pltpu.VMEM((feats + cyc, classes), F32),
        ],
        spectrum,
        cp,
        cid,
        ctf,
    )
    sums = exchange(sums, "dom")
    parts = call(
        regroup_kernel,
        shape((owners, 16, LANES), BF16),
        [pltpu.VMEM((feats // doms + cyc // doms, classes), F32)],
        sums,
    )
    parts = exchange(parts, "cls")
    return call(
        finish_kernel,
        shape((own, cyc // doms, ang), F32),
        [],
        parts,
        jnp.asarray(order, BF16),
    )


def solution(mesh):
    return jax.shard_map(
        on_device,
        mesh=mesh,
        in_specs=(
            P(("dom", "cls"), None, None),
            P("cls", None, None),
            P(),
            P(("dom", "cls")),
            P(("dom", "cls"), None),
        ),
        out_specs=P("cls", "dom", None),
        check_vma=False,
    )
```

```python
import numpy as np

import jax
import jax.numpy as jnp
from jax import lax
from jax.experimental import pallas as pl
from jax.experimental.pallas import tpu as pltpu
from jax.sharding import PartitionSpec as P

F32 = jnp.float32
BF16 = jnp.bfloat16
NT = (((1,), (1,)), ((), ()))
LANES = 128


def tables(angles, slices):
    harm = angles // 2
    per = harm // slices
    s, c, m = np.meshgrid(np.arange(slices), np.arange(2), np.arange(per), indexing="ij")
    harmonic = (s * per + m).reshape(-1)
    is_sin = c.reshape(-1)
    phase = (harmonic[:, None] * np.arange(angles)[None, :]) % angles
    grid = phase * (2.0 * np.pi / angles)
    cosine = np.cos(grid).astype(np.float32)
    sine = np.sin(grid).astype(np.float32)
    forward = np.where(is_sin[:, None] == 0, cosine, sine).astype(np.float32)
    weight = np.where(harmonic == 0, 1.0, 2.0).astype(np.float32) / angles
    inverse = (np.where(is_sin[:, None] == 0, cosine, -sine) * weight[:, None]).T.astype(np.float32)
    column = is_sin * harm + harmonic
    order = np.zeros((angles, angles), np.float32)
    order[np.arange(angles), column] = 1.0
    return forward, inverse, order


def lane_swap(arrays):
    n = len(arrays)
    width = LANES // n
    arrays = list(arrays)
    lane = lax.broadcasted_iota(jnp.int32, arrays[0].shape, 1)
    step = n // 2
    while step >= 1:
        shift = width * step
        low = (lane & shift) == 0
        for a in range(n):
            if a & step == 0:
                x, y = arrays[a], arrays[a + step]
                arrays[a] = jnp.where(low, x, pltpu.roll(y, shift, 1))
                arrays[a + step] = jnp.where(low, pltpu.roll(x, LANES - shift, 1), y)
        step //= 2
    return arrays


def harmonics_kernel(img_hbm, ref_hbm, pri_hbm, def_hbm, fwd_hbm, out_hbm, *scratch):
    img_ref, ref_ref, pri_ref, def_ref, fwd_ref, out_ref, img_s, ref_s, int_s, sems, out_sems = scratch
    n, cyc, ang = img_ref.shape
    own = ref_ref.shape[0]
    dest = out_ref.shape[0]
    half = cyc // 2
    pieces = 4
    span = cyc // pieces

    def piece(src, dst, k, sem):
        cut = pl.ds(k * span, span)
        return pltpu.make_async_copy(src.at[:, cut, :], dst.at[:, cut, :], sem)

    copies = [
        pltpu.make_async_copy(fwd_hbm, fwd_ref, sems.at[0]),
        pltpu.make_async_copy(pri_hbm, pri_ref, sems.at[1]),
        pltpu.make_async_copy(def_hbm, def_ref, sems.at[2]),
    ]
    refs = [piece(ref_hbm, ref_ref, k, sems.at[3 + k]) for k in range(pieces)]
    imgs = [piece(img_hbm, img_ref, k, sems.at[3 + pieces + k]) for k in range(pieces)]
    for copy in copies[:1] + refs + imgs + copies[1:]:
        copy.start()
    sent = []

    def send(column, width):
        cut = pl.ds(column, width)
        copy = pltpu.make_async_copy(
            out_ref.at[:, :, cut], out_hbm.at[:, :, cut], out_sems.at[len(sent)]
        )
        copy.start()
        sent.append(copy)

    def part(ref, src, count, column, arrivals):
        group = LANES // count
        steps = half // group
        for p in range(pieces):
            arrivals[p].wait()
            for k in range(ang // LANES):
                lanes = slice(k * LANES, (k + 1) * LANES)
                for i in range(count):
                    block = ref[i, p * span : (p + 1) * span, lanes].astype(F32)
                    src[k, i * cyc + p * span : i * cyc + (p + 1) * span] = block
            for c in range(p * steps // pieces, (p + 1) * steps // pieces):
                block = jnp.concatenate(
                    [
                        jnp.concatenate(
                            [
                                src[k, pl.ds(2 * (group * c + q) + odd, count, stride=cyc), :]
                                for odd in range(2)
                                for q in range(group)
                            ],
                            axis=0,
                        )
                        for k in range(ang // LANES)
                    ],
                    axis=1,
                ).astype(BF16)
                y = lax.dot_general(fwd_ref[...], block, NT, preferred_element_type=F32)
                y = y.reshape(dest, 8, 2 * LANES)
                y = jnp.concatenate([y[:, :, :LANES], y[:, :, LANES:]], axis=1)
                out_ref[:, :, column + c * LANES : column + (c + 1) * LANES] = y.astype(BF16)
            width = steps // pieces * LANES
            send(column + p * width, width)

    copies[0].wait()
    part(ref_ref, ref_s, own, half * n, refs)
    part(img_ref, img_s, n, 0, imgs)
    copies[1].wait()
    copies[2].wait()
    pri = pri_ref[...]
    int_s[...] = jnp.zeros_like(int_s)
    int_s[0:8, 0:n] = (pri // own).astype(F32)
    int_s[8:16, 0:n] = (pri - (pri // own) * own).astype(F32)
    int_s[0:1, n : 2 * n] = def_ref[...].astype(F32)
    column = half * (n + own)
    out_ref[:, :, column : column + LANES] = jnp.broadcast_to(
        int_s[...].astype(BF16)[None], (dest, 16, LANES)
    )
    send(column, LANES)
    for copy in sent:
        copy.wait()


def one_hot(row, count):
    index = lax.broadcasted_iota(jnp.int32, (count, row.shape[1]), 0)
    return jnp.where(index == row, 1.0, 0.0).astype(BF16)


def flip_rows(x):
    return pltpu.roll(x, 4, x.ndim - 2)


def score_kernel(own, in_ref, ctf_ref, x_ref, cp_ref, cq_ref, hot_ref, c_ref, cid_s, rt_s, x_s):
    src = in_ref.shape[0]
    groups, cyc = ctf_ref.shape
    half = cyc // 2
    total = cp_ref.shape[1]
    n = total // src
    col_r = half * n
    col_i = half * (n + own)
    per = LANES // n
    per_r = LANES // own
    blocks = src // per

    ctf_t = ctf_ref[...].T
    for b in range(blocks):
        lanes = slice(b * LANES, (b + 1) * LANES)
        v = lane_swap(
            [in_ref[per * b + i, :, col_i : col_i + LANES].astype(F32) for i in range(per)]
        )
        cid_s[:, lanes] = (v[0][0:8] * float(own) + v[0][8:16]).astype(jnp.int32)
        group = v[1][0:1].astype(jnp.int32)
        hot = (lax.broadcasted_iota(jnp.int32, (groups, LANES), 0) == group).astype(F32)
        c_ref[:, lanes] = jnp.dot(
            ctf_t, hot, precision=lax.Precision.HIGHEST, preferred_element_type=F32
        )

    def unpack_r(c, carry):
        col = pl.multiple_of(col_r + c * LANES, LANES)
        for b in range(src // per_r):
            v = lane_swap(
                [in_ref[per_r * b + i, :, pl.ds(col, LANES)].astype(F32) for i in range(per_r)]
            )
            for q in range(per_r):
                row = pl.multiple_of((per_r * c + q) * 16, 16)
                rt_s[pl.ds(row, 16), b * LANES : (b + 1) * LANES] = v[q].astype(BF16)
        return carry

    lax.fori_loop(0, half // per_r, unpack_r, 0)

    upper = lax.broadcasted_iota(jnp.int32, (16, LANES), 0) % 8 >= 4

    def unpack_p(c, carry):
        col = pl.multiple_of(c * LANES, LANES)
        for b in range(blocks):
            lanes = slice(b * LANES, (b + 1) * LANES)
            v = lane_swap(
                [in_ref[per * b + i, :, pl.ds(col, LANES)].astype(F32) for i in range(per)]
            )
            ctf = c_ref[pl.ds(pl.multiple_of(c * 2 * per, 2 * per), 2 * per), lanes]
            for q in range(per):
                row = pl.multiple_of((per * c + q) * 16, 16)
                scale = jnp.concatenate(
                    [
                        jnp.broadcast_to(ctf[2 * q + odd : 2 * q + odd + 1], (8, LANES))
                        for odd in range(2)
                    ],
                    axis=0,
                )
                p = v[q] * scale
                cp_ref[pl.ds(row, 16), lanes] = p
                swapped = flip_rows(p.reshape(2, 8, LANES)).reshape(16, LANES)
                cq_ref[pl.ds(row, 16), lanes] = jnp.where(upper, swapped, -swapped)
        return carry

    lax.fori_loop(0, half // per, unpack_p, 0)

    chunks, classes, wide = hot_ref.shape
    wide = wide // 8
    low = lax.broadcasted_iota(jnp.int32, (8, wide), 0) < 4

    def chunk(t, carry):
        col = pl.multiple_of(t * wide, wide)
        cols = pl.ds(col, wide)
        for j in range(8):
            hot = one_hot(cid_s[j : j + 1, cols], classes)
            hot_ref[t, :, j * wide : (j + 1) * wide] = hot
            picked = jnp.dot(rt_s[...], hot, preferred_element_type=F32)
            re = jnp.sum((cp_ref[:, cols] * picked).reshape(cyc, 8, wide), axis=0)
            im = jnp.sum((cq_ref[:, cols] * picked).reshape(cyc, 8, wide), axis=0)
            x_s[j, :, cols] = jnp.where(low, re + flip_rows(re), im + flip_rows(im))
        return carry

    lax.fori_loop(0, chunks, chunk, 0)

    for b in range(blocks):
        lanes = slice(b * LANES, (b + 1) * LANES)
        for u in range(8 // per):
            v = lane_swap([x_s[per * u + j, :, lanes] for j in range(per)])
            for i in range(per):
                x_ref[per * b + i, :, u * LANES : (u + 1) * LANES] = v[i]


def weight_kernel(x_ref, inv_ref, fwd_ref, out_ref):
    src, rows, slots = x_ref.shape
    high = lax.Precision.HIGHEST
    x = x_ref[...].reshape(src * rows, slots)
    score = jnp.dot(inv_ref[...], x, precision=high, preferred_element_type=F32)

    def over_slots(row, op):
        row = op(row[:, :LANES], row[:, LANES:])
        row = op(row, pltpu.roll(row, 64, 1))
        row = op(row, pltpu.roll(row, 32, 1))
        return jnp.concatenate([row, row], axis=1)

    top = jnp.broadcast_to(jnp.max(score, axis=0, keepdims=True), (8, slots))
    top = over_slots(top, jnp.maximum)[0:1]
    grown = jnp.exp(score - top)
    part = jnp.broadcast_to(jnp.sum(grown, axis=0, keepdims=True), (8, slots))
    inverse = 1.0 / over_slots(part, jnp.add)
    weight = grown * inverse[0:1]
    spectrum = jnp.dot(fwd_ref[...], weight, precision=high, preferred_element_type=F32)
    out_ref[...] = spectrum.reshape(src, rows, slots).astype(out_ref.dtype)


def sum_kernel(w_ref, cp_ref, cq_ref, hot_ref, c_ref, out_ref, w_s, t_s, sum_s):
    src = w_ref.shape[0]
    feats, total = cp_ref.shape
    chunks, classes, wide = hot_ref.shape
    wide = wide // 8
    cyc = feats // 8
    n = total // src
    per = LANES // n
    for b in range(src // per):
        lanes = slice(b * LANES, (b + 1) * LANES)
        for u in range(8 // per):
            v = lane_swap(
                [w_ref[per * b + i, :, u * LANES : (u + 1) * LANES].astype(F32) for i in range(per)]
            )
            for j in range(per):
                w_s[per * u + j, :, lanes] = v[j]

    low = lax.broadcasted_iota(jnp.int32, (8, wide), 0) < 4
    for t in range(chunks):
        cols = slice(t * wide, (t + 1) * wide)
        for j in range(8):
            w = w_s[j, :, cols]
            turned = flip_rows(w)
            wc = jnp.where(low, w, turned)
            ws = jnp.where(low, turned, w)
            p = cp_ref[:, cols].reshape(cyc, 8, wide)
            q = cq_ref[:, cols].reshape(cyc, 8, wide)
            term = p * wc[None] - q * ws[None]
            slot = slice(j * wide, (j + 1) * wide)
            t_s[t % 2, 0:feats, slot] = term.reshape(feats, wide).astype(BF16)
            c = c_ref[:, cols]
            t_s[t % 2, feats:, slot] = (c * c * w[0:1]).astype(BF16)
        part = lax.dot_general(t_s[t % 2], hot_ref[t], NT, preferred_element_type=F32)
        if t == 0:
            sum_s[...] = part
        else:
            sum_s[...] += part
    own = classes // src
    per = LANES // own
    rows = 8 * per
    for d in range(feats // rows):
        for b in range(classes // LANES):
            lanes = slice(b * LANES, (b + 1) * LANES)
            v = lane_swap([sum_s[d * rows + 8 * q : d * rows + 8 * q + 8, lanes] for q in range(per)])
            norm = sum_s[feats + d * per : feats + (d + 1) * per, lanes]
            norm = lane_swap([jnp.broadcast_to(norm[q : q + 1], (8, LANES)) for q in range(per)])
            for k in range(per):
                part = v[k].astype(BF16)
                to = d * src + per * b + k
                for g in range(4):
                    out_ref[to, :, g * LANES : (g + 1) * LANES] = part[2 * g : 2 * g + 2]
                out_ref[to, :, 4 * LANES :] = norm[k][0:2].astype(BF16)


def finish_kernel(in_ref, order_ref, out_ref):
    own, part, width = out_ref.shape
    every = in_ref.shape[0]
    src = width // 8
    x = jnp.zeros((width, LANES), F32)
    for g in range(4):
        rows = in_ref[:, :, g * LANES : (g + 1) * LANES].reshape(2 * every, LANES)
        x += jnp.dot(order_ref[g], rows, preferred_element_type=F32)
    norm = in_ref[0, :, 4 * LANES :].astype(F32)
    for d in range(1, every // src):
        norm += in_ref[d * src, :, 4 * LANES :].astype(F32)
    x = jnp.concatenate([x, jnp.broadcast_to(norm[0:1], (8, LANES))], axis=0)
    a = lax.broadcasted_iota(jnp.int32, (LANES, LANES), 0)
    b = lax.broadcasted_iota(jnp.int32, (LANES, LANES), 1)
    turn = jnp.where((a % own) * part + a // own == b, 1.0, 0.0)
    x = jnp.dot(x, turn, precision=lax.Precision.HIGHEST, preferred_element_type=F32).T
    out_ref[...] = (x[:, :width] / (x[:, width : width + 1] + 1.0)).reshape(own, part, width)


def call(kernel, shapes, scratch, *args, space=pltpu.VMEM, limit=24):
    many = isinstance(shapes, (list, tuple)) and not hasattr(shapes, "dtype")
    spec = pl.BlockSpec(memory_space=space)
    return pl.pallas_call(
        kernel,
        out_shape=shapes,
        in_specs=[pl.BlockSpec(memory_space=space)] * len(args),
        out_specs=[spec] * len(shapes) if many else spec,
        scratch_shapes=scratch,
        compiler_params=pltpu.CompilerParams(vmem_limit_bytes=limit << 20),
    )(*args)


def on_device(images, references, ctf_table, defocus, priors):
    owners = lax.axis_size("cls")
    doms = lax.axis_size("dom")
    n, cyc, ang = images.shape
    own = references.shape[0]
    total = owners * n
    classes = owners * own
    feats = 8 * cyc
    wide = 256
    forward, inverse, order = tables(ang, owners)
    pairs = order.reshape(owners, 4, 2, ang).transpose(1, 3, 0, 2).reshape(4, ang, 2 * owners)
    pairs = np.tile(pairs, (1, 1, doms))
    shape = jax.ShapeDtypeStruct
    pri = priors.T
    group = defocus.reshape(1, n)

    def exchange(x, axis):
        return lax.all_to_all(x, axis, split_axis=0, concat_axis=0, tiled=True)

    width = (cyc // 2) * (n + own) + LANES
    sent = call(
        harmonics_kernel,
        shape((owners, 16, width), BF16),
        [
            pltpu.VMEM((n, cyc, ang), BF16),
            pltpu.VMEM((own, cyc, ang), BF16),
            pltpu.VMEM((8, n), jnp.int32),
            pltpu.VMEM((1, n), jnp.int32),
            pltpu.VMEM((ang, ang), BF16),
            pltpu.VMEM((owners, 16, width), BF16),
            pltpu.VMEM((ang // LANES, n * cyc, LANES), F32),
            pltpu.VMEM((ang // LANES, own * cyc, LANES), F32),
            pltpu.VMEM((16, LANES), F32),
            pltpu.SemaphoreType.DMA((11,)),
            pltpu.SemaphoreType.DMA((9,)),
        ],
        images,
        references,
        pri,
        group,
        jnp.asarray(forward, BF16),
        space=pltpu.HBM,
        limit=60,
    )
    got = exchange(sent, "cls")
    x, cp, cq, hot, ctf = call(
        lambda *refs: score_kernel(own, *refs),
        [
            shape((owners, 8, 8 * n), F32),
            shape((feats, total), F32),
            shape((feats, total), F32),
            shape((total // wide, classes, 8 * wide), BF16),
            shape((cyc, total), F32),
        ],
        [
            pltpu.VMEM((8, total), jnp.int32),
            pltpu.VMEM((feats, classes), BF16),
            pltpu.VMEM((8, 8, total), F32),
        ],
        got,
        ctf_table,
    )
    x = exchange(x, "cls")
    spectrum = call(
        weight_kernel,
        shape((owners, 8, 8 * n), BF16),
        [],
        x,
        jnp.asarray(inverse),
        jnp.asarray(forward),
    )
    spectrum = exchange(spectrum, "cls")
    sums = call(
        sum_kernel,
        shape((doms * owners, 2, 5 * LANES), BF16),
        [
            pltpu.VMEM((8, 8, total), F32),
            pltpu.VMEM((2, feats + cyc, 8 * wide), BF16),
            pltpu.VMEM((feats + cyc, classes), F32),
        ],
        spectrum,
        cp,
        cq,
        hot,
        ctf,
    )
    sums = exchange(sums, ("dom", "cls"))
    return call(
        finish_kernel,
        shape((own, cyc // doms, ang), F32),
        [],
        sums,
        jnp.asarray(pairs, BF16),
    )


def solution(mesh):
    return jax.shard_map(
        on_device,
        mesh=mesh,
        in_specs=(
            P(("dom", "cls"), None, None),
            P("cls", None, None),
            P(),
            P(("dom", "cls")),
            P(("dom", "cls"), None),
        ),
        out_specs=P("cls", "dom", None),
        check_vma=False,
    )
```

```python
import numpy as np

import jax
import jax.numpy as jnp
from jax import lax
from jax.experimental import pallas as pl
from jax.experimental.pallas import tpu as pltpu
from jax.sharding import PartitionSpec as P

F32 = jnp.float32
BF16 = jnp.bfloat16
NT = (((1,), (1,)), ((), ()))
LANES = 128


def tables(angles, slices):
    harm = angles // 2
    per = harm // slices
    s, c, m = np.meshgrid(np.arange(slices), np.arange(2), np.arange(per), indexing="ij")
    harmonic = (s * per + m).reshape(-1)
    is_sin = c.reshape(-1)
    phase = (harmonic[:, None] * np.arange(angles)[None, :]) % angles
    grid = phase * (2.0 * np.pi / angles)
    cosine = np.cos(grid).astype(np.float32)
    sine = np.sin(grid).astype(np.float32)
    forward = np.where(is_sin[:, None] == 0, cosine, sine).astype(np.float32)
    weight = np.where(harmonic == 0, 1.0, 2.0).astype(np.float32) / angles
    inverse = (np.where(is_sin[:, None] == 0, cosine, -sine) * weight[:, None]).T.astype(np.float32)
    column = is_sin * harm + harmonic
    order = np.zeros((angles, angles), np.float32)
    order[np.arange(angles), column] = 1.0
    return forward, inverse, order


def lane_swap(arrays):
    n = len(arrays)
    width = LANES // n
    arrays = list(arrays)
    lane = lax.broadcasted_iota(jnp.int32, arrays[0].shape, 1)
    step = n // 2
    while step >= 1:
        shift = width * step
        low = (lane & shift) == 0
        for a in range(n):
            if a & step == 0:
                x, y = arrays[a], arrays[a + step]
                arrays[a] = jnp.where(low, x, pltpu.roll(y, shift, 1))
                arrays[a + step] = jnp.where(low, pltpu.roll(x, LANES - shift, 1), y)
        step //= 2
    return arrays


def harmonics_kernel(img_hbm, ref_hbm, pri_hbm, def_hbm, fwd_hbm, out_ref, *scratch):
    img_ref, ref_ref, pri_ref, def_ref, fwd_ref, img_s, ref_s, int_s, sems = scratch
    n, cyc, ang = img_ref.shape
    own = ref_ref.shape[0]
    dest = out_ref.shape[0]
    pairs = (
        (fwd_hbm, fwd_ref),
        (ref_hbm, ref_ref),
        (img_hbm, img_ref),
        (pri_hbm, pri_ref),
        (def_hbm, def_ref),
    )
    copies = [pltpu.make_async_copy(a, b, sems.at[k]) for k, (a, b) in enumerate(pairs)]
    for copy in copies:
        copy.start()

    def part(ref, src, count, column):
        for k in range(ang // LANES):
            src[k] = ref[:, :, k * LANES : (k + 1) * LANES].astype(F32).reshape(count * cyc, LANES)
        wide = 2 * LANES
        group = wide // count
        for c in range(cyc // group):
            block = jnp.concatenate(
                [
                    jnp.concatenate(
                        [src[k, pl.ds(group * c + q, count, stride=cyc), :] for q in range(group)],
                        axis=0,
                    )
                    for k in range(ang // LANES)
                ],
                axis=1,
            ).astype(BF16)
            y = lax.dot_general(fwd_ref[...], block, NT, preferred_element_type=F32)
            cut = slice(column + c * wide, column + (c + 1) * wide)
            out_ref[:, :, cut] = y.reshape(dest, 8, wide).astype(BF16)

    copies[3].wait()
    copies[4].wait()
    int_s[...] = jnp.zeros_like(int_s)
    int_s[:, 0:n] = (pri_ref[...] - dest * own // 2).astype(F32)
    int_s[0:1, n : 2 * n] = def_ref[...].astype(F32)
    column = cyc * (n + own)
    out_ref[:, :, column : column + LANES] = jnp.broadcast_to(
        int_s[...].astype(BF16)[None], (dest, 8, LANES)
    )
    copies[0].wait()
    copies[1].wait()
    part(ref_ref, ref_s, own, cyc * n)
    copies[2].wait()
    part(img_ref, img_s, n, 0)


def one_hot(row, count):
    wide = row.shape[1]
    index = lax.broadcasted_iota(jnp.int32, (count, wide), 0).astype(jnp.int16)
    row = jnp.broadcast_to(row, (16, wide)).astype(jnp.int16)
    hot = index.reshape(count // 16, 16, wide) == row[None]
    return jnp.where(hot, jnp.ones((), BF16), jnp.zeros((), BF16)).reshape(count, wide)


def flip_rows(x):
    return pltpu.roll(x, 4, x.ndim - 2)


def score_kernel(own, in_ref, ctf_ref, x_ref, cp_ref, cq_ref, hot_ref, c_ref, cid_s, rt_s, x_s):
    src = in_ref.shape[0]
    groups, cyc = ctf_ref.shape
    total = cp_ref.shape[1]
    n = total // src
    col_r = cyc * n
    col_i = cyc * (n + own)
    per = LANES // n
    per_r = LANES // own
    blocks = src // per

    ctf_t = ctf_ref[...].T
    for b in range(blocks):
        lanes = slice(b * LANES, (b + 1) * LANES)
        v = lane_swap(
            [in_ref[per * b + i, :, col_i : col_i + LANES].astype(F32) for i in range(per)]
        )
        cid_s[:, lanes] = v[0].astype(jnp.int32) + src * own // 2
        group = v[1][0:1].astype(jnp.int32)
        hot = (lax.broadcasted_iota(jnp.int32, (groups, LANES), 0) == group).astype(F32)
        c_ref[:, lanes] = jnp.dot(
            ctf_t, hot, precision=lax.Precision.HIGHEST, preferred_element_type=F32
        )

    def unpack_r(c, carry):
        col = pl.multiple_of(col_r + c * LANES, LANES)
        for b in range(src // per_r):
            v = lane_swap(
                [in_ref[per_r * b + i, :, pl.ds(col, LANES)].astype(F32) for i in range(per_r)]
            )
            for q in range(0, per_r, 2):
                row = pl.multiple_of((per_r * c + q) * 8, 16)
                pair = jnp.concatenate([v[q], v[q + 1]], axis=0)
                rt_s[pl.ds(row, 16), b * LANES : (b + 1) * LANES] = pair.astype(BF16)
        return carry

    lax.fori_loop(0, cyc // per_r, unpack_r, 0)

    upper = lax.broadcasted_iota(jnp.int32, (8, LANES), 0) >= 4

    def unpack_p(c, carry):
        for b in range(blocks):
            lanes = slice(b * LANES, (b + 1) * LANES)
            ctf = c_ref[pl.ds(pl.multiple_of(c * 2 * per, 2 * per), 2 * per), lanes]
            for part in range(2):
                col = pl.multiple_of((2 * c + part) * LANES, LANES)
                v = lane_swap(
                    [in_ref[per * b + i, :, pl.ds(col, LANES)].astype(F32) for i in range(per)]
                )
                for q in range(per):
                    r = per * part + q
                    row = pl.multiple_of((2 * per * c + r) * 8, 8)
                    p = v[q] * jnp.broadcast_to(ctf[r : r + 1], (8, LANES))
                    cp_ref[pl.ds(row, 8), lanes] = p
                    swapped = flip_rows(p)
                    cq_ref[pl.ds(row, 8), lanes] = jnp.where(upper, swapped, -swapped)
        return carry

    lax.fori_loop(0, cyc // (2 * per), unpack_p, 0)

    chunks, classes, wide = hot_ref.shape
    wide = wide // 8
    low = lax.broadcasted_iota(jnp.int32, (8, wide), 0) < 4

    for t in range(chunks):
        cols = slice(t * wide, (t + 1) * wide)
        for j in range(8):
            hot = one_hot(cid_s[j : j + 1, cols], classes)
            hot_ref[t, :, j * wide : (j + 1) * wide] = hot
            picked = jnp.dot(rt_s[...], hot, preferred_element_type=F32)
            re = jnp.sum((cp_ref[:, cols] * picked).reshape(cyc, 8, wide), axis=0)
            im = jnp.sum((cq_ref[:, cols] * picked).reshape(cyc, 8, wide), axis=0)
            x_s[j, :, cols] = jnp.where(low, re + flip_rows(re), im + flip_rows(im))

    for b in range(blocks):
        lanes = slice(b * LANES, (b + 1) * LANES)
        for u in range(8 // per):
            v = lane_swap([x_s[per * u + j, :, lanes] for j in range(per)])
            for i in range(per):
                x_ref[per * b + i, :, u * LANES : (u + 1) * LANES] = v[i]


def weight_kernel(x_ref, inv_ref, fwd_ref, out_ref):
    src, rows, slots = x_ref.shape
    high = lax.Precision.HIGHEST
    x = x_ref[...].reshape(src * rows, slots)
    score = jnp.dot(inv_ref[...], x, precision=high, preferred_element_type=F32)

    def over_slots(row, op):
        row = op(row[:, :LANES], row[:, LANES:])
        row = op(row, pltpu.roll(row, 64, 1))
        row = op(row, pltpu.roll(row, 32, 1))
        return jnp.concatenate([row, row], axis=1)

    top = jnp.broadcast_to(jnp.max(score, axis=0, keepdims=True), (8, slots))
    top = over_slots(top, jnp.maximum)[0:1]
    grown = jnp.exp(score - top)
    part = jnp.broadcast_to(jnp.sum(grown, axis=0, keepdims=True), (8, slots))
    inverse = 1.0 / over_slots(part, jnp.add)
    weight = grown * inverse[0:1]
    spectrum = jnp.dot(fwd_ref[...], weight, precision=high, preferred_element_type=F32)
    out_ref[...] = spectrum.reshape(src, rows, slots).astype(out_ref.dtype)


def sum_kernel(w_ref, cp_ref, cq_ref, hot_ref, c_ref, out_ref, w_s, t_s, sum_s):
    src = w_ref.shape[0]
    feats, total = cp_ref.shape
    chunks, classes, wide = hot_ref.shape
    wide = wide // 8
    cyc = feats // 8
    n = total // src
    per = LANES // n
    for b in range(src // per):
        lanes = slice(b * LANES, (b + 1) * LANES)
        for u in range(8 // per):
            v = lane_swap(
                [w_ref[per * b + i, :, u * LANES : (u + 1) * LANES].astype(F32) for i in range(per)]
            )
            for j in range(per):
                w_s[per * u + j, :, lanes] = v[j]

    low = lax.broadcasted_iota(jnp.int32, (8, wide), 0) < 4
    for t in range(chunks):
        cols = slice(t * wide, (t + 1) * wide)
        for j in range(8):
            w = w_s[j, :, cols]
            turned = flip_rows(w)
            wc = jnp.where(low, w, turned)
            ws = jnp.where(low, turned, w)
            p = cp_ref[:, cols].reshape(cyc, 8, wide)
            q = cq_ref[:, cols].reshape(cyc, 8, wide)
            term = p * wc[None] - q * ws[None]
            slot = slice(j * wide, (j + 1) * wide)
            t_s[t % 2, 0:feats, slot] = term.reshape(feats, wide).astype(BF16)
            c = c_ref[:, cols]
            t_s[t % 2, feats:, slot] = (c * c * w[0:1]).astype(BF16)
        part = lax.dot_general(t_s[t % 2], hot_ref[t], NT, preferred_element_type=F32)
        if t == 0:
            sum_s[...] = part
        else:
            sum_s[...] += part
    own = classes // src
    per = LANES // own
    rows = 8 * per
    for d in range(feats // rows):
        for b in range(classes // LANES):
            lanes = slice(b * LANES, (b + 1) * LANES)
            v = lane_swap([sum_s[d * rows + 8 * q : d * rows + 8 * q + 8, lanes] for q in range(per)])
            norm = sum_s[feats + d * per : feats + (d + 1) * per, lanes]
            norm = lane_swap([jnp.broadcast_to(norm[q : q + 1], (8, LANES)) for q in range(per)])
            for k in range(per):
                part = v[k].astype(BF16)
                to = d * src + per * b + k
                for g in range(4):
                    out_ref[to, :, g * LANES : (g + 1) * LANES] = part[2 * g : 2 * g + 2]
                out_ref[to, :, 4 * LANES :] = norm[k][0:2].astype(BF16)


def finish_kernel(in_ref, order_ref, out_ref, out_s):
    own, part, width = out_ref.shape
    every = in_ref.shape[0]
    src = width // 8
    x = jnp.zeros((width, LANES), F32)
    for g in range(4):
        rows = in_ref[:, :, g * LANES : (g + 1) * LANES].reshape(2 * every, LANES)
        x += jnp.dot(order_ref[g], rows, preferred_element_type=F32)
    norm = in_ref[0, :, 4 * LANES :].astype(F32)
    for d in range(1, every // src):
        norm += in_ref[d * src, :, 4 * LANES :].astype(F32)
    x = jnp.concatenate([x, jnp.broadcast_to(norm[0:1], (8, LANES))], axis=0)
    x = x.T
    x = x[:, :width] / (x[:, width : width + 1] + 1.0)
    for q in range(part):
        for k in range(width // LANES):
            lanes = slice(k * LANES, (k + 1) * LANES)
            out_s[k, pl.ds(q, own, stride=part), :] = x[q * own : (q + 1) * own, lanes]
    for k in range(width // LANES):
        out_ref[:, :, k * LANES : (k + 1) * LANES] = out_s[k].reshape(own, part, LANES)


def call(kernel, shapes, scratch, *args, space=pltpu.VMEM, limit=24):
    many = isinstance(shapes, (list, tuple)) and not hasattr(shapes, "dtype")
    spec = pl.BlockSpec(memory_space=pltpu.VMEM)
    return pl.pallas_call(
        kernel,
        out_shape=shapes,
        in_specs=[pl.BlockSpec(memory_space=space)] * len(args),
        out_specs=[spec] * len(shapes) if many else spec,
        scratch_shapes=scratch,
        compiler_params=pltpu.CompilerParams(vmem_limit_bytes=limit << 20),
    )(*args)


def on_device(images, references, ctf_table, defocus, priors):
    owners = lax.axis_size("cls")
    doms = lax.axis_size("dom")
    n, cyc, ang = images.shape
    own = references.shape[0]
    total = owners * n
    classes = owners * own
    feats = 8 * cyc
    wide = 256
    forward, inverse, order = tables(ang, owners)
    pairs = order.reshape(owners, 4, 2, ang).transpose(1, 3, 0, 2).reshape(4, ang, 2 * owners)
    pairs = np.tile(pairs, (1, 1, doms))
    shape = jax.ShapeDtypeStruct
    pri = priors.T
    group = defocus.reshape(1, n)

    def exchange(x, axis):
        return lax.all_to_all(x, axis, split_axis=0, concat_axis=0, tiled=True)

    width = cyc * (n + own) + LANES
    sent = call(
        harmonics_kernel,
        shape((owners, 8, width), BF16),
        [
            pltpu.VMEM((n, cyc, ang), BF16),
            pltpu.VMEM((own, cyc, ang), BF16),
            pltpu.VMEM((8, n), jnp.int32),
            pltpu.VMEM((1, n), jnp.int32),
            pltpu.VMEM((ang, ang), BF16),
            pltpu.VMEM((ang // LANES, n * cyc, LANES), F32),
            pltpu.VMEM((ang // LANES, own * cyc, LANES), F32),
            pltpu.VMEM((8, LANES), F32),
            pltpu.SemaphoreType.DMA((5,)),
        ],
        *[pltpu.with_memory_space_constraint(x, pltpu.HBM) for x in (images, references, pri, group)],
        pltpu.with_memory_space_constraint(jnp.asarray(forward, BF16), pltpu.HBM),
        space=pltpu.HBM,
    )
    got = exchange(sent, "cls")
    x, cp, cq, hot, ctf = call(
        lambda *refs: score_kernel(own, *refs),
        [
            shape((owners, 8, 8 * n), F32),
            shape((feats, total), F32),
            shape((feats, total), F32),
            shape((total // wide, classes, 8 * wide), BF16),
            shape((cyc, total), F32),
        ],
        [
            pltpu.VMEM((8, total), jnp.int32),
            pltpu.VMEM((feats, classes), BF16),
            pltpu.VMEM((8, 8, total), F32),
        ],
        got,
        ctf_table,
    )
    x = exchange(x, "cls")
    spectrum = call(
        weight_kernel,
        shape((owners, 8, 8 * n), BF16),
        [],
        x,
        jnp.asarray(inverse),
        jnp.asarray(forward),
    )
    spectrum = exchange(spectrum, "cls")
    sums = call(
        sum_kernel,
        shape((doms * owners, 2, 5 * LANES), BF16),
        [
            pltpu.VMEM((8, 8, total), F32),
            pltpu.VMEM((2, feats + cyc, 8 * wide), BF16),
            pltpu.VMEM((feats + cyc, classes), F32),
        ],
        spectrum,
        cp,
        cq,
        hot,
        ctf,
    )
    sums = exchange(sums, ("dom", "cls"))
    return call(
        finish_kernel,
        shape((own, cyc // doms, ang), F32),
        [pltpu.VMEM((ang // LANES, own * cyc // doms, LANES), F32)],
        sums,
        jnp.asarray(pairs, BF16),
    )


def solution(mesh):
    return jax.shard_map(
        on_device,
        mesh=mesh,
        in_specs=(
            P(("dom", "cls"), None, None),
            P("cls", None, None),
            P(),
            P(("dom", "cls")),
            P(("dom", "cls"), None),
        ),
        out_specs=P("cls", "dom", None),
        check_vma=False,
    )
```

```python
import numpy as np

import jax
import jax.numpy as jnp
from jax import lax
from jax.experimental import pallas as pl
from jax.experimental.pallas import tpu as pltpu
from jax.sharding import PartitionSpec as P

F32 = jnp.float32
BF16 = jnp.bfloat16
NT = (((1,), (1,)), ((), ()))
LANES = 128


def tables(angles, slices):
    harm = angles // 2
    per = harm // slices
    s, c, m = np.meshgrid(np.arange(slices), np.arange(2), np.arange(per), indexing="ij")
    harmonic = (s * per + m).reshape(-1)
    is_sin = c.reshape(-1)
    phase = (harmonic[:, None] * np.arange(angles)[None, :]) % angles
    grid = phase * (2.0 * np.pi / angles)
    cosine = np.cos(grid).astype(np.float32)
    sine = np.sin(grid).astype(np.float32)
    forward = np.where(is_sin[:, None] == 0, cosine, sine).astype(np.float32)
    weight = np.where(harmonic == 0, 1.0, 2.0).astype(np.float32) / angles
    inverse = (np.where(is_sin[:, None] == 0, cosine, -sine) * weight[:, None]).T.astype(np.float32)
    column = is_sin * harm + harmonic
    order = np.zeros((angles, angles), np.float32)
    order[np.arange(angles), column] = 1.0
    return forward, inverse, order


def swap_table(count):
    size = count * LANES
    to = np.arange(size).reshape(count, count, LANES // count).transpose(1, 0, 2).reshape(-1)
    table = np.zeros((size, size), np.float32)
    table[to, np.arange(size)] = 1.0
    return jnp.asarray(table, BF16)


def lane_swap(arrays):
    n = len(arrays)
    width = LANES // n
    arrays = list(arrays)
    lane = lax.broadcasted_iota(jnp.int32, arrays[0].shape, 1)
    step = n // 2
    while step >= 1:
        shift = width * step
        low = (lane & shift) == 0
        for a in range(n):
            if a & step == 0:
                x, y = arrays[a], arrays[a + step]
                arrays[a] = jnp.where(low, x, pltpu.roll(y, shift, 1))
                arrays[a + step] = jnp.where(low, pltpu.roll(x, LANES - shift, 1), y)
        step //= 2
    return arrays


def harmonics_kernel(img_hbm, ref_hbm, pri_hbm, def_hbm, fwd_hbm, out_ref, *scratch):
    img_ref, ref_ref, pri_ref, def_ref, fwd_ref, img_s, ref_s, int_s, sems = scratch
    n, cyc, ang = img_ref.shape
    own = ref_ref.shape[0]
    dest = out_ref.shape[0]
    rows_p = 8 * cyc * n // LANES
    rows_r = 8 * cyc * own // LANES
    pairs = (
        (fwd_hbm, fwd_ref),
        (ref_hbm, ref_ref),
        (img_hbm, img_ref),
        (pri_hbm, pri_ref),
        (def_hbm, def_ref),
    )
    copies = [pltpu.make_async_copy(a, b, sems.at[k]) for k, (a, b) in enumerate(pairs)]
    for copy in copies:
        copy.start()

    def part(ref, src, count, start):
        for k in range(ang // LANES):
            src[k] = ref[:, :, k * LANES : (k + 1) * LANES].astype(F32).reshape(count * cyc, LANES)
        wide = 2 * LANES
        group = wide // count
        for c in range(cyc // group):
            block = jnp.concatenate(
                [
                    jnp.concatenate(
                        [src[k, pl.ds(group * c + q, count, stride=cyc), :] for q in range(group)],
                        axis=0,
                    )
                    for k in range(ang // LANES)
                ],
                axis=1,
            ).astype(BF16)
            y = lax.dot_general(fwd_ref[...], block, NT, preferred_element_type=F32)
            y = y.reshape(dest, 8, wide)
            y = jnp.concatenate([y[:, :, :LANES], y[:, :, LANES:]], axis=1)
            out_ref[:, start + 16 * c : start + 16 * (c + 1), :] = y.astype(BF16)

    copies[3].wait()
    copies[4].wait()
    int_s[...] = jnp.zeros_like(int_s)
    int_s[:, 0:n] = (pri_ref[...] - dest * own // 2).astype(F32)
    int_s[0:1, n : 2 * n] = def_ref[...].astype(F32)
    out_ref[:, (rows_p + rows_r) :, :] = jnp.broadcast_to(
        int_s[...].astype(BF16)[None], (dest, 8, LANES)
    )
    copies[0].wait()
    copies[1].wait()
    part(ref_ref, ref_s, own, rows_p)
    copies[2].wait()
    part(img_ref, img_s, n, 0)


def one_hot(row, count):
    wide = row.shape[1]
    index = lax.broadcasted_iota(jnp.int32, (count, wide), 0).astype(jnp.int16)
    row = jnp.broadcast_to(row, (16, wide)).astype(jnp.int16)
    hot = index.reshape(count // 16, 16, wide) == row[None]
    return jnp.where(hot, jnp.ones((), BF16), jnp.zeros((), BF16)).reshape(count, wide)


def flip_rows(x):
    return pltpu.roll(x, 4, x.ndim - 2)


def score_kernel(own, in_ref, ctf_ref, swap_p_ref, swap_r_ref, x_ref, cp_ref, cq_ref, hot_ref, c_ref, cid_s, rt_s, x_s):
    src = in_ref.shape[0]
    groups, cyc = ctf_ref.shape
    total = cp_ref.shape[1]
    n = total // src
    rows_p = 8 * cyc * n // LANES
    rows_r = 8 * cyc * own // LANES
    per = LANES // n
    per_r = LANES // own
    blocks = src // per

    ctf_t = ctf_ref[...].T
    for b in range(blocks):
        lanes = slice(b * LANES, (b + 1) * LANES)
        v = lane_swap(
            [in_ref[per * b + i, (rows_p + rows_r) :, :].astype(F32) for i in range(per)]
        )
        cid_s[:, lanes] = v[0].astype(jnp.int32) + src * own // 2
        group = v[1][0:1].astype(jnp.int32)
        hot = (lax.broadcasted_iota(jnp.int32, (groups, LANES), 0) == group).astype(F32)
        c_ref[:, lanes] = jnp.dot(
            ctf_t, hot, precision=lax.Precision.HIGHEST, preferred_element_type=F32
        )

    def swapped(first, last, size, table):
        blocks = [
            jnp.concatenate([in_ref[b + i, first:last, :] for i in range(size)], axis=1)
            for b in range(0, src, size)
        ]
        return jnp.dot(jnp.concatenate(blocks, axis=0), table[...], preferred_element_type=F32)

    every = swapped(rows_p, rows_p + rows_r, per_r, swap_r_ref).astype(BF16)
    for b in range(src // per_r):
        y = every[b * rows_r : (b + 1) * rows_r].reshape(rows_r // 8, 8, per_r * LANES)
        for c in range(rows_r // 8):
            for q in range(0, per_r, 2):
                pair = [y[c, :, (q + k) * LANES : (q + k + 1) * LANES] for k in range(2)]
                row = (per_r * c + q) * 8
                rt_s[row : row + 16, b * LANES : (b + 1) * LANES] = jnp.concatenate(pair, axis=0)

    upper = lax.broadcasted_iota(jnp.int32, (8, LANES), 0) >= 4
    every = swapped(0, rows_p, per, swap_p_ref)
    for b in range(blocks):
        lanes = slice(b * LANES, (b + 1) * LANES)
        y = every[b * rows_p : (b + 1) * rows_p]
        ctf = c_ref[:, lanes]
        for c in range(rows_p // 8):
            for q in range(per):
                r = per * c + q
                p = y[8 * c : 8 * c + 8, q * LANES : (q + 1) * LANES]
                p = p * jnp.broadcast_to(ctf[r : r + 1], (8, LANES))
                cp_ref[8 * r : 8 * r + 8, lanes] = p
                turned = flip_rows(p)
                cq_ref[8 * r : 8 * r + 8, lanes] = jnp.where(upper, turned, -turned)

    chunks, classes, wide = hot_ref.shape
    wide = wide // 8
    low = lax.broadcasted_iota(jnp.int32, (8, wide), 0) < 4

    for t in range(chunks):
        cols = slice(t * wide, (t + 1) * wide)
        for j in range(8):
            hot = one_hot(cid_s[j : j + 1, cols], classes)
            hot_ref[t, :, j * wide : (j + 1) * wide] = hot
            picked = jnp.dot(rt_s[...], hot, preferred_element_type=F32)
            re = jnp.sum((cp_ref[:, cols] * picked).reshape(cyc, 8, wide), axis=0)
            im = jnp.sum((cq_ref[:, cols] * picked).reshape(cyc, 8, wide), axis=0)
            x_s[j, :, cols] = jnp.where(low, re + flip_rows(re), im + flip_rows(im))

    for b in range(blocks):
        lanes = slice(b * LANES, (b + 1) * LANES)
        for u in range(8 // per):
            v = lane_swap([x_s[per * u + j, :, lanes] for j in range(per)])
            for i in range(per):
                x_ref[per * b + i, :, u * LANES : (u + 1) * LANES] = v[i]


def weight_kernel(x_ref, inv_ref, fwd_ref, out_ref):
    src, rows, slots = x_ref.shape
    high = lax.Precision.HIGHEST
    x = x_ref[...].reshape(src * rows, slots)
    score = jnp.dot(inv_ref[...], x, precision=high, preferred_element_type=F32)

    def over_slots(row, op):
        row = op(row[:, :LANES], row[:, LANES:])
        row = op(row, pltpu.roll(row, 64, 1))
        row = op(row, pltpu.roll(row, 32, 1))
        return jnp.concatenate([row, row], axis=1)

    top = jnp.broadcast_to(jnp.max(score, axis=0, keepdims=True), (8, slots))
    top = over_slots(top, jnp.maximum)[0:1]
    grown = jnp.exp(score - top)
    part = jnp.broadcast_to(jnp.sum(grown, axis=0, keepdims=True), (8, slots))
    inverse = 1.0 / over_slots(part, jnp.add)
    weight = grown * inverse[0:1]
    spectrum = jnp.dot(fwd_ref[...], weight, precision=high, preferred_element_type=F32)
    out_ref[...] = spectrum.reshape(src, rows, slots).astype(out_ref.dtype)


def sum_kernel(w_ref, cp_ref, cq_ref, hot_ref, c_ref, out_ref, w_s, t_s, sum_s):
    src = w_ref.shape[0]
    feats, total = cp_ref.shape
    chunks, classes, wide = hot_ref.shape
    wide = wide // 8
    cyc = feats // 8
    n = total // src
    per = LANES // n
    for b in range(src // per):
        lanes = slice(b * LANES, (b + 1) * LANES)
        for u in range(8 // per):
            v = lane_swap(
                [w_ref[per * b + i, :, u * LANES : (u + 1) * LANES].astype(F32) for i in range(per)]
            )
            for j in range(per):
                w_s[per * u + j, :, lanes] = v[j]

    low = lax.broadcasted_iota(jnp.int32, (8, wide), 0) < 4
    for t in range(chunks):
        cols = slice(t * wide, (t + 1) * wide)
        for j in range(8):
            w = w_s[j, :, cols]
            turned = flip_rows(w)
            wc = jnp.where(low, w, turned)
            ws = jnp.where(low, turned, w)
            p = cp_ref[:, cols].reshape(cyc, 8, wide)
            q = cq_ref[:, cols].reshape(cyc, 8, wide)
            term = p * wc[None] - q * ws[None]
            slot = slice(j * wide, (j + 1) * wide)
            t_s[t % 2, 0:feats, slot] = term.reshape(feats, wide).astype(BF16)
            c = c_ref[:, cols]
            t_s[t % 2, feats:, slot] = (c * c * w[0:1]).astype(BF16)
        part = lax.dot_general(t_s[t % 2], hot_ref[t], NT, preferred_element_type=F32)
        if t == 0:
            sum_s[...] = part
        else:
            sum_s[...] += part
    own = classes // src
    per = LANES // own
    rows = 8 * per
    for d in range(feats // rows):
        for b in range(classes // LANES):
            lanes = slice(b * LANES, (b + 1) * LANES)
            v = lane_swap([sum_s[d * rows + 8 * q : d * rows + 8 * q + 8, lanes] for q in range(per)])
            norm = sum_s[feats + d * per : feats + (d + 1) * per, lanes]
            norm = lane_swap([jnp.broadcast_to(norm[q : q + 1], (8, LANES)) for q in range(per)])
            for k in range(per):
                part = v[k].astype(BF16)
                to = d * src + per * b + k
                for g in range(4):
                    out_ref[to, :, g * LANES : (g + 1) * LANES] = part[2 * g : 2 * g + 2]
                out_ref[to, :, 4 * LANES :] = norm[k][0:2].astype(BF16)


def finish_kernel(in_ref, order_ref, out_ref, out_s):
    own, part, width = out_ref.shape
    every = in_ref.shape[0]
    src = width // 8
    x = jnp.zeros((width, LANES), F32)
    for g in range(4):
        rows = in_ref[:, :, g * LANES : (g + 1) * LANES].reshape(2 * every, LANES)
        x += jnp.dot(order_ref[g], rows, preferred_element_type=F32)
    norm = in_ref[0, :, 4 * LANES :].astype(F32)
    for d in range(1, every // src):
        norm += in_ref[d * src, :, 4 * LANES :].astype(F32)
    x = jnp.concatenate([x, jnp.broadcast_to(norm[0:1], (8, LANES))], axis=0)
    x = x.T
    x = x[:, :width] / (x[:, width : width + 1] + 1.0)
    for q in range(part):
        for k in range(width // LANES):
            lanes = slice(k * LANES, (k + 1) * LANES)
            out_s[k, pl.ds(q, own, stride=part), :] = x[q * own : (q + 1) * own, lanes]
    for k in range(width // LANES):
        out_ref[:, :, k * LANES : (k + 1) * LANES] = out_s[k].reshape(own, part, LANES)


def call(kernel, shapes, scratch, *args, space=pltpu.VMEM, limit=24):
    many = isinstance(shapes, (list, tuple)) and not hasattr(shapes, "dtype")
    spec = pl.BlockSpec(memory_space=pltpu.VMEM)
    return pl.pallas_call(
        kernel,
        out_shape=shapes,
        in_specs=[pl.BlockSpec(memory_space=space)] * len(args),
        out_specs=[spec] * len(shapes) if many else spec,
        scratch_shapes=scratch,
        compiler_params=pltpu.CompilerParams(vmem_limit_bytes=limit << 20),
    )(*args)


def on_device(images, references, ctf_table, defocus, priors):
    owners = lax.axis_size("cls")
    doms = lax.axis_size("dom")
    n, cyc, ang = images.shape
    own = references.shape[0]
    total = owners * n
    classes = owners * own
    feats = 8 * cyc
    wide = 256
    forward, inverse, order = tables(ang, owners)
    pairs = order.reshape(owners, 4, 2, ang).transpose(1, 3, 0, 2).reshape(4, ang, 2 * owners)
    pairs = np.tile(pairs, (1, 1, doms))
    shape = jax.ShapeDtypeStruct
    pri = priors.T
    group = defocus.reshape(1, n)

    def exchange(x, axis):
        return lax.all_to_all(x, axis, split_axis=0, concat_axis=0, tiled=True)

    rows = 8 * (cyc * (n + own) // LANES + 1)
    sent = call(
        harmonics_kernel,
        shape((owners, rows, LANES), BF16),
        [
            pltpu.VMEM((n, cyc, ang), BF16),
            pltpu.VMEM((own, cyc, ang), BF16),
            pltpu.VMEM((8, n), jnp.int32),
            pltpu.VMEM((1, n), jnp.int32),
            pltpu.VMEM((ang, ang), BF16),
            pltpu.VMEM((ang // LANES, n * cyc, LANES), F32),
            pltpu.VMEM((ang // LANES, own * cyc, LANES), F32),
            pltpu.VMEM((8, LANES), F32),
            pltpu.SemaphoreType.DMA((5,)),
        ],
        *[pltpu.with_memory_space_constraint(x, pltpu.HBM) for x in (images, references, pri, group)],
        pltpu.with_memory_space_constraint(jnp.asarray(forward, BF16), pltpu.HBM),
        space=pltpu.HBM,
    )
    got = exchange(sent, "cls")
    x, cp, cq, hot, ctf = call(
        lambda *refs: score_kernel(own, *refs),
        [
            shape((owners, 8, 8 * n), F32),
            shape((feats, total), F32),
            shape((feats, total), F32),
            shape((total // wide, classes, 8 * wide), BF16),
            shape((cyc, total), F32),
        ],
        [
            pltpu.VMEM((8, total), jnp.int32),
            pltpu.VMEM((feats, classes), BF16),
            pltpu.VMEM((8, 8, total), F32),
        ],
        got,
        ctf_table,
        swap_table(LANES // n),
        swap_table(LANES // own),
    )
    x = exchange(x, "cls")
    spectrum = call(
        weight_kernel,
        shape((owners, 8, 8 * n), BF16),
        [],
        x,
        jnp.asarray(inverse),
        jnp.asarray(forward),
    )
    spectrum = exchange(spectrum, "cls")
    sums = call(
        sum_kernel,
        shape((doms * owners, 2, 5 * LANES), BF16),
        [
            pltpu.VMEM((8, 8, total), F32),
            pltpu.VMEM((2, feats + cyc, 8 * wide), BF16),
            pltpu.VMEM((feats + cyc, classes), F32),
        ],
        spectrum,
        cp,
        cq,
        hot,
        ctf,
    )
    sums = exchange(sums, ("dom", "cls"))
    return call(
        finish_kernel,
        shape((own, cyc // doms, ang), F32),
        [pltpu.VMEM((ang // LANES, own * cyc // doms, LANES), F32)],
        sums,
        jnp.asarray(pairs, BF16),
    )


def solution(mesh):
    return jax.shard_map(
        on_device,
        mesh=mesh,
        in_specs=(
            P(("dom", "cls"), None, None),
            P("cls", None, None),
            P(),
            P(("dom", "cls")),
            P(("dom", "cls"), None),
        ),
        out_specs=P("cls", "dom", None),
        check_vma=False,
    )
```

```python
import numpy as np

import jax
import jax.numpy as jnp
from jax import lax
from jax.experimental import pallas as pl
from jax.experimental.pallas import tpu as pltpu
from jax.sharding import PartitionSpec as P

F32 = jnp.float32
BF16 = jnp.bfloat16
NT = (((1,), (1,)), ((), ()))
LANES = 128


def tables(angles, slices):
    harm = angles // 2
    per = harm // slices
    s, c, m = np.meshgrid(np.arange(slices), np.arange(2), np.arange(per), indexing="ij")
    harmonic = (s * per + m).reshape(-1)
    is_sin = c.reshape(-1)
    phase = (harmonic[:, None] * np.arange(angles)[None, :]) % angles
    grid = phase * (2.0 * np.pi / angles)
    cosine = np.cos(grid).astype(np.float32)
    sine = np.sin(grid).astype(np.float32)
    forward = np.where(is_sin[:, None] == 0, cosine, sine).astype(np.float32)
    weight = np.where(harmonic == 0, 1.0, 2.0).astype(np.float32) / angles
    inverse = (np.where(is_sin[:, None] == 0, cosine, -sine) * weight[:, None]).T.astype(np.float32)
    column = is_sin * harm + harmonic
    order = np.zeros((angles, angles), np.float32)
    order[np.arange(angles), column] = 1.0
    return forward, inverse, order


def swap_table(count):
    size = count * LANES
    to = np.arange(size).reshape(count, count, LANES // count).transpose(1, 0, 2).reshape(-1)
    table = np.zeros((size, size), np.float32)
    table[to, np.arange(size)] = 1.0
    return jnp.asarray(table, BF16)


def lane_swap(arrays):
    n = len(arrays)
    width = LANES // n
    arrays = list(arrays)
    lane = lax.broadcasted_iota(jnp.int32, arrays[0].shape, 1)
    step = n // 2
    while step >= 1:
        shift = width * step
        low = (lane & shift) == 0
        for a in range(n):
            if a & step == 0:
                x, y = arrays[a], arrays[a + step]
                arrays[a] = jnp.where(low, x, pltpu.roll(y, shift, 1))
                arrays[a + step] = jnp.where(low, pltpu.roll(x, LANES - shift, 1), y)
        step //= 2
    return arrays


def harmonics_kernel(img_hbm, ref_hbm, pri_hbm, def_hbm, fwd_hbm, out_ref, *scratch):
    img_ref, ref_ref, pri_ref, def_ref, fwd_ref, img_s, ref_s, int_s, sems = scratch
    n, cyc, ang = img_ref.shape
    own = ref_ref.shape[0]
    dest = out_ref.shape[0]
    rows_p = 8 * cyc * n // LANES
    rows_r = 8 * cyc * own // LANES
    pairs = (
        (fwd_hbm, fwd_ref),
        (ref_hbm, ref_ref),
        (img_hbm, img_ref),
        (pri_hbm, pri_ref),
        (def_hbm, def_ref),
    )
    copies = [pltpu.make_async_copy(a, b, sems.at[k]) for k, (a, b) in enumerate(pairs)]
    for copy in copies:
        copy.start()

    def part(ref, src, count, start):
        for k in range(ang // LANES):
            src[k] = ref[:, :, k * LANES : (k + 1) * LANES].astype(F32).reshape(count * cyc, LANES)
        wide = 2 * LANES
        group = wide // count
        for c in range(cyc // group):
            block = jnp.concatenate(
                [
                    jnp.concatenate(
                        [src[k, pl.ds(group * c + q, count, stride=cyc), :] for q in range(group)],
                        axis=0,
                    )
                    for k in range(ang // LANES)
                ],
                axis=1,
            ).astype(BF16)
            y = lax.dot_general(fwd_ref[...], block, NT, preferred_element_type=F32)
            y = y.reshape(dest, 8, wide)
            y = jnp.concatenate([y[:, :, :LANES], y[:, :, LANES:]], axis=1)
            out_ref[:, start + 16 * c : start + 16 * (c + 1), :] = y.astype(BF16)

    copies[3].wait()
    copies[4].wait()
    int_s[...] = jnp.zeros_like(int_s)
    int_s[:, 0:n] = (pri_ref[...] - dest * own // 2).astype(F32)
    int_s[0:1, n : 2 * n] = def_ref[...].astype(F32)
    out_ref[:, (rows_p + rows_r) :, :] = jnp.broadcast_to(
        int_s[...].astype(BF16)[None], (dest, 8, LANES)
    )
    copies[0].wait()
    copies[1].wait()
    part(ref_ref, ref_s, own, rows_p)
    copies[2].wait()
    part(img_ref, img_s, n, 0)


def one_hot(row, count):
    wide = row.shape[1]
    index = lax.broadcasted_iota(jnp.int32, (count, wide), 0).astype(jnp.int16)
    row = jnp.broadcast_to(row, (16, wide)).astype(jnp.int16)
    hot = index.reshape(count // 16, 16, wide) == row[None]
    return jnp.where(hot, jnp.ones((), BF16), jnp.zeros((), BF16)).reshape(count, wide)


def flip_rows(x):
    return pltpu.roll(x, 4, x.ndim - 2)


def score_kernel(own, in_ref, ctf_ref, swap_p_ref, swap_r_ref, x_ref, cp_ref, cq_ref, hot_ref, c_ref, cid_s, rt_s, x_s):
    src = in_ref.shape[0]
    groups, cyc = ctf_ref.shape
    total = cp_ref.shape[1]
    n = total // src
    rows_p = 8 * cyc * n // LANES
    rows_r = 8 * cyc * own // LANES
    per = LANES // n
    per_r = LANES // own
    blocks = src // per

    ctf_t = ctf_ref[...].T
    for b in range(blocks):
        lanes = slice(b * LANES, (b + 1) * LANES)
        v = lane_swap(
            [in_ref[per * b + i, (rows_p + rows_r) :, :].astype(F32) for i in range(per)]
        )
        cid_s[:, lanes] = v[0].astype(jnp.int32) + src * own // 2
        group = v[1][0:1].astype(jnp.int32)
        hot = (lax.broadcasted_iota(jnp.int32, (groups, LANES), 0) == group).astype(F32)
        c_ref[:, lanes] = jnp.dot(
            ctf_t, hot, precision=lax.Precision.HIGHEST, preferred_element_type=F32
        )

    def swapped(first, last, size, table):
        blocks = [
            jnp.concatenate([in_ref[b + i, first:last, :] for i in range(size)], axis=1)
            for b in range(0, src, size)
        ]
        return jnp.dot(jnp.concatenate(blocks, axis=0), table[...], preferred_element_type=F32)

    every = swapped(rows_p, rows_p + rows_r, per_r, swap_r_ref).astype(BF16)
    for b in range(src // per_r):
        y = every[b * rows_r : (b + 1) * rows_r].reshape(rows_r // 8, 8, per_r * LANES)
        for c in range(rows_r // 8):
            for q in range(0, per_r, 2):
                pair = [y[c, :, (q + k) * LANES : (q + k + 1) * LANES] for k in range(2)]
                row = (per_r * c + q) * 8
                rt_s[row : row + 16, b * LANES : (b + 1) * LANES] = jnp.concatenate(pair, axis=0)

    upper = lax.broadcasted_iota(jnp.int32, (8, LANES), 0) >= 4
    every = swapped(0, rows_p, per, swap_p_ref)
    for b in range(blocks):
        lanes = slice(b * LANES, (b + 1) * LANES)
        y = every[b * rows_p : (b + 1) * rows_p]
        ctf = c_ref[:, lanes]
        for c in range(rows_p // 8):
            for q in range(per):
                r = per * c + q
                p = y[8 * c : 8 * c + 8, q * LANES : (q + 1) * LANES]
                p = p * jnp.broadcast_to(ctf[r : r + 1], (8, LANES))
                cp_ref[8 * r : 8 * r + 8, lanes] = p
                turned = flip_rows(p)
                cq_ref[8 * r : 8 * r + 8, lanes] = jnp.where(upper, turned, -turned)

    chunks, classes, wide = hot_ref.shape
    wide = wide // 8
    low = lax.broadcasted_iota(jnp.int32, (8, wide), 0) < 4

    for t in range(chunks):
        cols = slice(t * wide, (t + 1) * wide)
        for j in range(8):
            hot = one_hot(cid_s[j : j + 1, cols], classes)
            hot_ref[t, :, j * wide : (j + 1) * wide] = hot
            picked = jnp.dot(rt_s[...], hot, preferred_element_type=F32)
            re = jnp.sum((cp_ref[:, cols] * picked).reshape(cyc, 8, wide), axis=0)
            im = jnp.sum((cq_ref[:, cols] * picked).reshape(cyc, 8, wide), axis=0)
            x_s[j, :, cols] = jnp.where(low, re + flip_rows(re), im + flip_rows(im))

    for b in range(blocks):
        lanes = slice(b * LANES, (b + 1) * LANES)
        for u in range(8 // per):
            v = lane_swap([x_s[per * u + j, :, lanes] for j in range(per)])
            for i in range(per):
                x_ref[per * b + i, :, u * LANES : (u + 1) * LANES] = v[i]


def weight_kernel(x_ref, inv_ref, fwd_ref, out_ref):
    src, rows, slots = x_ref.shape
    high = lax.Precision.HIGHEST
    x = x_ref[...].reshape(src * rows, slots)
    score = jnp.dot(inv_ref[...], x, precision=high, preferred_element_type=F32)

    def over_slots(row, op):
        row = op(row[:, :LANES], row[:, LANES:])
        row = op(row, pltpu.roll(row, 64, 1))
        row = op(row, pltpu.roll(row, 32, 1))
        return jnp.concatenate([row, row], axis=1)

    top = jnp.broadcast_to(jnp.max(score, axis=0, keepdims=True), (8, slots))
    top = over_slots(top, jnp.maximum)[0:1]
    grown = jnp.exp(score - top)
    part = jnp.broadcast_to(jnp.sum(grown, axis=0, keepdims=True), (8, slots))
    inverse = 1.0 / over_slots(part, jnp.add)
    weight = grown * inverse[0:1]
    spectrum = jnp.dot(
        fwd_ref[...], weight, precision=lax.Precision.HIGH, preferred_element_type=F32
    )
    out_ref[...] = spectrum.reshape(src, rows, slots).astype(out_ref.dtype)


def sum_kernel(w_ref, cp_ref, cq_ref, hot_ref, c_ref, out_ref, w_s, t_s, sum_s, norm_s):
    src = w_ref.shape[0]
    feats, total = cp_ref.shape
    chunks, classes, wide = hot_ref.shape
    wide = wide // 8
    cyc = feats // 8
    n = total // src
    per = LANES // n
    for b in range(src // per):
        lanes = slice(b * LANES, (b + 1) * LANES)
        for u in range(8 // per):
            v = lane_swap(
                [w_ref[per * b + i, :, u * LANES : (u + 1) * LANES].astype(F32) for i in range(per)]
            )
            for j in range(per):
                w_s[per * u + j, :, lanes] = v[j]

    low = lax.broadcasted_iota(jnp.int32, (8, wide), 0) < 4
    own = classes // src
    per = LANES // own
    doms = cyc // per
    halves = sum_s.shape[0]
    span = feats // halves
    some = cyc // halves
    for h in range(halves):
        rows = slice(h * span, (h + 1) * span)
        for t in range(chunks):
            cols = slice(t * wide, (t + 1) * wide)
            buf = t % 2
            for j in range(8):
                w = w_s[j, :, cols]
                turned = flip_rows(w)
                wc = jnp.where(low, w, turned)
                ws = jnp.where(low, turned, w)
                p = cp_ref[rows, cols].reshape(some, 8, wide)
                q = cq_ref[rows, cols].reshape(some, 8, wide)
                term = p * wc[None] - q * ws[None]
                slot = slice(j * wide, (j + 1) * wide)
                t_s[h, buf, 0:span, slot] = term.reshape(span, wide).astype(BF16)
                c = c_ref[h * some : (h + 1) * some, cols]
                t_s[h, buf, span:, slot] = (c * c * w[0:1]).astype(BF16)
            part = lax.dot_general(t_s[h, buf], hot_ref[t], NT, preferred_element_type=F32)
            if t == 0:
                sum_s[h] = part
            else:
                sum_s[h] += part
        norms = []
        for b in range(classes // LANES):
            norm_s[h, b] = sum_s[h, span:, b * LANES : (b + 1) * LANES]
            rows_q = [norm_s[h, b, pl.ds(q, doms // halves, stride=per), :] for q in range(per)]
            norms.append(lane_swap(rows_q))
        for d in range(doms // halves):
            for b in range(classes // LANES):
                lanes = slice(b * LANES, (b + 1) * LANES)
                v = [sum_s[h, 8 * (d * per + q) : 8 * (d * per + q) + 8, lanes] for q in range(per)]
                v = lane_swap(v)
                for k in range(per):
                    part = v[k].astype(BF16)
                    to = (h * doms // halves + d) * src + per * b + k
                    for g in range(4):
                        out_ref[to, :, g * LANES : (g + 1) * LANES] = part[2 * g : 2 * g + 2]
                    norm = jnp.broadcast_to(norms[b][k][d : d + 1], (2, LANES))
                    out_ref[to, :, 4 * LANES :] = norm.astype(BF16)


def finish_kernel(in_ref, order_ref, out_ref, out_s):
    own, part, width = out_ref.shape
    every = in_ref.shape[0]
    src = width // 8
    x = jnp.zeros((width, LANES), F32)
    for g in range(4):
        rows = in_ref[:, :, g * LANES : (g + 1) * LANES].reshape(2 * every, LANES)
        x += jnp.dot(order_ref[g], rows, preferred_element_type=F32)
    norm = in_ref[0, :, 4 * LANES :].astype(F32)
    for d in range(1, every // src):
        norm += in_ref[d * src, :, 4 * LANES :].astype(F32)
    x = jnp.concatenate([x, jnp.broadcast_to(norm[0:1], (8, LANES))], axis=0)
    x = x.T
    x = x[:, :width] / (x[:, width : width + 1] + 1.0)
    for q in range(part):
        for k in range(width // LANES):
            lanes = slice(k * LANES, (k + 1) * LANES)
            out_s[k, pl.ds(q, own, stride=part), :] = x[q * own : (q + 1) * own, lanes]
    for k in range(width // LANES):
        out_ref[:, :, k * LANES : (k + 1) * LANES] = out_s[k].reshape(own, part, LANES)


def call(kernel, shapes, scratch, *args, space=pltpu.VMEM, limit=24):
    many = isinstance(shapes, (list, tuple)) and not hasattr(shapes, "dtype")
    spec = pl.BlockSpec(memory_space=pltpu.VMEM)
    return pl.pallas_call(
        kernel,
        out_shape=shapes,
        in_specs=[pl.BlockSpec(memory_space=space)] * len(args),
        out_specs=[spec] * len(shapes) if many else spec,
        scratch_shapes=scratch,
        compiler_params=pltpu.CompilerParams(vmem_limit_bytes=limit << 20),
    )(*args)


def on_device(images, references, ctf_table, defocus, priors):
    owners = lax.axis_size("cls")
    doms = lax.axis_size("dom")
    n, cyc, ang = images.shape
    own = references.shape[0]
    total = owners * n
    classes = owners * own
    feats = 8 * cyc
    wide = 256
    forward, inverse, order = tables(ang, owners)
    pairs = order.reshape(owners, 4, 2, ang).transpose(1, 3, 0, 2).reshape(4, ang, 2 * owners)
    pairs = np.tile(pairs, (1, 1, doms))
    shape = jax.ShapeDtypeStruct
    pri = priors.T
    group = defocus.reshape(1, n)

    def exchange(x, axis):
        return lax.all_to_all(x, axis, split_axis=0, concat_axis=0, tiled=True)

    rows = 8 * (cyc * (n + own) // LANES + 1)
    sent = call(
        harmonics_kernel,
        shape((owners, rows, LANES), BF16),
        [
            pltpu.VMEM((n, cyc, ang), BF16),
            pltpu.VMEM((own, cyc, ang), BF16),
            pltpu.VMEM((8, n), jnp.int32),
            pltpu.VMEM((1, n), jnp.int32),
            pltpu.VMEM((ang, ang), BF16),
            pltpu.VMEM((ang // LANES, n * cyc, LANES), F32),
            pltpu.VMEM((ang // LANES, own * cyc, LANES), F32),
            pltpu.VMEM((8, LANES), F32),
            pltpu.SemaphoreType.DMA((5,)),
        ],
        *[pltpu.with_memory_space_constraint(x, pltpu.HBM) for x in (images, references, pri, group)],
        pltpu.with_memory_space_constraint(jnp.asarray(forward, BF16), pltpu.HBM),
        space=pltpu.HBM,
    )
    got = exchange(sent, "cls")
    x, cp, cq, hot, ctf = call(
        lambda *refs: score_kernel(own, *refs),
        [
            shape((owners, 8, 8 * n), F32),
            shape((feats, total), F32),
            shape((feats, total), F32),
            shape((total // wide, classes, 8 * wide), BF16),
            shape((cyc, total), F32),
        ],
        [
            pltpu.VMEM((8, total), jnp.int32),
            pltpu.VMEM((feats, classes), BF16),
            pltpu.VMEM((8, 8, total), F32),
        ],
        got,
        ctf_table,
        swap_table(LANES // n),
        swap_table(LANES // own),
    )
    x = exchange(x, "cls")
    spectrum = call(
        weight_kernel,
        shape((owners, 8, 8 * n), BF16),
        [],
        x,
        jnp.asarray(inverse),
        jnp.asarray(forward),
    )
    spectrum = exchange(spectrum, "cls")
    sums = call(
        sum_kernel,
        shape((doms * owners, 2, 5 * LANES), BF16),
        [
            pltpu.VMEM((8, 8, total), F32),
            pltpu.VMEM((2, 2, (feats + cyc) // 2, 8 * wide), BF16),
            pltpu.VMEM((2, (feats + cyc) // 2, classes), F32),
            pltpu.VMEM((2, classes // LANES, cyc // 2, LANES), F32),
        ],
        spectrum,
        cp,
        cq,
        hot,
        ctf,
    )
    sums = exchange(sums, ("dom", "cls"))
    return call(
        finish_kernel,
        shape((own, cyc // doms, ang), F32),
        [pltpu.VMEM((ang // LANES, own * cyc // doms, LANES), F32)],
        sums,
        jnp.asarray(pairs, BF16),
    )


def solution(mesh):
    return jax.shard_map(
        on_device,
        mesh=mesh,
        in_specs=(
            P(("dom", "cls"), None, None),
            P("cls", None, None),
            P(),
            P(("dom", "cls")),
            P(("dom", "cls"), None),
        ),
        out_specs=P("cls", "dom", None),
        check_vma=False,
    )
```

```python
import numpy as np

import jax
import jax.numpy as jnp
from jax import lax
from jax.experimental import pallas as pl
from jax.experimental.pallas import tpu as pltpu
from jax.sharding import PartitionSpec as P

F32 = jnp.float32
BF16 = jnp.bfloat16
NT = (((1,), (1,)), ((), ()))
LANES = 128


def tables(angles, slices):
    harm = angles // 2
    per = harm // slices
    s, c, m = np.meshgrid(np.arange(slices), np.arange(2), np.arange(per), indexing="ij")
    harmonic = (s * per + m).reshape(-1)
    is_sin = c.reshape(-1)
    phase = (harmonic[:, None] * np.arange(angles)[None, :]) % angles
    grid = phase * (2.0 * np.pi / angles)
    cosine = np.cos(grid).astype(np.float32)
    sine = np.sin(grid).astype(np.float32)
    forward = np.where(is_sin[:, None] == 0, cosine, sine).astype(np.float32)
    weight = np.where(harmonic == 0, 1.0, 2.0).astype(np.float32) / angles
    inverse = (np.where(is_sin[:, None] == 0, cosine, -sine) * weight[:, None]).T.astype(np.float32)
    column = is_sin * harm + harmonic
    order = np.zeros((angles, angles), np.float32)
    order[np.arange(angles), column] = 1.0
    return forward, inverse, order


def swap_table(count):
    size = count * LANES
    to = np.arange(size).reshape(count, count, LANES // count).transpose(1, 0, 2).reshape(-1)
    table = np.zeros((size, size), np.float32)
    table[to, np.arange(size)] = 1.0
    return jnp.asarray(table, BF16)


def lane_swap(arrays):
    n = len(arrays)
    width = LANES // n
    arrays = list(arrays)
    lane = lax.broadcasted_iota(jnp.int32, arrays[0].shape, 1)
    step = n // 2
    while step >= 1:
        shift = width * step
        low = (lane & shift) == 0
        for a in range(n):
            if a & step == 0:
                x, y = arrays[a], arrays[a + step]
                arrays[a] = jnp.where(low, x, pltpu.roll(y, shift, 1))
                arrays[a + step] = jnp.where(low, pltpu.roll(x, LANES - shift, 1), y)
        step //= 2
    return arrays


def harmonics_kernel(img_hbm, ref_hbm, pri_hbm, def_hbm, fwd_hbm, out_ref, *scratch):
    img_ref, ref_ref, pri_ref, def_ref, fwd_ref, img_s, ref_s, int_s, sems = scratch
    n, cyc, ang = img_ref.shape
    own = ref_ref.shape[0]
    dest = out_ref.shape[0]
    rows_p = 8 * cyc * n // LANES
    rows_r = 8 * cyc * own // LANES
    pairs = (
        (fwd_hbm, fwd_ref),
        (ref_hbm, ref_ref),
        (img_hbm, img_ref),
        (pri_hbm, pri_ref),
        (def_hbm, def_ref),
    )
    copies = [pltpu.make_async_copy(a, b, sems.at[k]) for k, (a, b) in enumerate(pairs)]
    for copy in copies:
        copy.start()

    def part(ref, src, count, start):
        for k in range(ang // LANES):
            src[k] = ref[:, :, k * LANES : (k + 1) * LANES].astype(F32).reshape(count * cyc, LANES)
        wide = 2 * LANES
        group = wide // count
        for c in range(cyc // group):
            block = jnp.concatenate(
                [
                    jnp.concatenate(
                        [src[k, pl.ds(group * c + q, count, stride=cyc), :] for q in range(group)],
                        axis=0,
                    )
                    for k in range(ang // LANES)
                ],
                axis=1,
            ).astype(BF16)
            y = lax.dot_general(fwd_ref[...], block, NT, preferred_element_type=F32)
            y = y.reshape(dest, 8, wide)
            y = jnp.concatenate([y[:, :, :LANES], y[:, :, LANES:]], axis=1)
            out_ref[:, start + 16 * c : start + 16 * (c + 1), :] = y.astype(BF16)

    copies[3].wait()
    copies[4].wait()
    int_s[...] = jnp.zeros_like(int_s)
    int_s[:, 0:n] = (pri_ref[...] - dest * own // 2).astype(F32)
    int_s[0:1, n : 2 * n] = def_ref[...].astype(F32)
    out_ref[:, (rows_p + rows_r) :, :] = jnp.broadcast_to(
        int_s[...].astype(BF16)[None], (dest, 8, LANES)
    )
    copies[0].wait()
    copies[1].wait()
    part(ref_ref, ref_s, own, rows_p)
    copies[2].wait()
    part(img_ref, img_s, n, 0)


def one_hot(row, count):
    wide = row.shape[1]
    index = lax.broadcasted_iota(jnp.int32, (count, wide), 0).astype(jnp.int16)
    row = jnp.broadcast_to(row, (16, wide)).astype(jnp.int16)
    hot = index.reshape(count // 16, 16, wide) == row[None]
    return jnp.where(hot, jnp.ones((), BF16), jnp.zeros((), BF16)).reshape(count, wide)


def flip_rows(x):
    return pltpu.roll(x, 4, x.ndim - 2)


def score_kernel(own, in_ref, ctf_ref, swap_p_ref, swap_r_ref, x_ref, cp_ref, cq_ref, hot_ref, c_ref, cid_s, rt_s, x_s):
    src = in_ref.shape[0]
    groups, cyc = ctf_ref.shape
    total = cp_ref.shape[1]
    n = total // src
    rows_p = 8 * cyc * n // LANES
    rows_r = 8 * cyc * own // LANES
    per = LANES // n
    per_r = LANES // own
    blocks = src // per

    ctf = ctf_ref[...]
    parts = []
    for _ in range(3):
        parts.append(ctf.astype(BF16).astype(F32))
        ctf = ctf - parts[-1]
    parts = jnp.concatenate(parts, axis=0).T.astype(BF16)
    hots = []
    for b in range(blocks):
        lanes = slice(b * LANES, (b + 1) * LANES)
        v = lane_swap(
            [in_ref[per * b + i, (rows_p + rows_r) :, :].astype(F32) for i in range(per)]
        )
        cid_s[:, lanes] = v[0].astype(jnp.int32) + src * own // 2
        group = v[1][0:1].astype(jnp.int32)
        hots.append((lax.broadcasted_iota(jnp.int32, (groups, LANES), 0) == group).astype(F32))
    hots = jnp.concatenate(hots, axis=1)
    hots = jnp.concatenate([hots] * 3, axis=0).astype(BF16)
    c_ref[...] = jnp.dot(parts, hots, preferred_element_type=F32)

    def swapped(sources, first, last, size, table):
        blocks = [
            jnp.concatenate([in_ref[b + i, first:last, :] for i in range(size)], axis=1)
            for b in range(sources.start, sources.stop, size)
        ]
        return jnp.dot(jnp.concatenate(blocks, axis=0), table[...], preferred_element_type=F32)

    every = swapped(range(src), rows_p, rows_p + rows_r, per_r, swap_r_ref).astype(BF16)
    for b in range(src // per_r):
        y = every[b * rows_r : (b + 1) * rows_r].reshape(rows_r // 8, 8, per_r * LANES)
        for c in range(rows_r // 8):
            for q in range(0, per_r, 2):
                pair = [y[c, :, (q + k) * LANES : (q + k + 1) * LANES] for k in range(2)]
                row = (per_r * c + q) * 8
                rt_s[row : row + 16, b * LANES : (b + 1) * LANES] = jnp.concatenate(pair, axis=0)

    upper = lax.broadcasted_iota(jnp.int32, (8, LANES), 0) >= 4

    def scale(b, y):
        lanes = slice(b * LANES, (b + 1) * LANES)
        ctf = c_ref[:, lanes]
        for c in range(rows_p // 8):
            for q in range(per):
                r = per * c + q
                p = y[8 * c : 8 * c + 8, q * LANES : (q + 1) * LANES]
                p = p * jnp.broadcast_to(ctf[r : r + 1], (8, LANES))
                cp_ref[8 * r : 8 * r + 8, lanes] = p
                turned = flip_rows(p)
                cq_ref[8 * r : 8 * r + 8, lanes] = jnp.where(upper, turned, -turned)

    chunks, classes, wide = hot_ref.shape
    wide = wide // 8
    low = lax.broadcasted_iota(jnp.int32, (8, wide), 0) < 4

    for t in range(chunks):
        cols = slice(t * wide, (t + 1) * wide)
        if t % 2 == 0:
            sources = range(t * wide // n, (t + 2) * wide // n)
            every = swapped(sources, 0, rows_p, per, swap_p_ref)
        for b in range(wide // LANES):
            at = (t % 2 * wide // LANES + b) * rows_p
            scale(t * wide // LANES + b, every[at : at + rows_p])
        for j in range(8):
            hot = one_hot(cid_s[j : j + 1, cols], classes)
            hot_ref[t, :, j * wide : (j + 1) * wide] = hot
            picked = jnp.dot(rt_s[...], hot, preferred_element_type=F32)
            re = jnp.sum((cp_ref[:, cols] * picked).reshape(cyc, 8, wide), axis=0)
            im = jnp.sum((cq_ref[:, cols] * picked).reshape(cyc, 8, wide), axis=0)
            x_s[j, :, cols] = jnp.where(low, re + flip_rows(re), im + flip_rows(im))

    for b in range(blocks):
        lanes = slice(b * LANES, (b + 1) * LANES)
        for u in range(8 // per):
            v = lane_swap([x_s[per * u + j, :, lanes] for j in range(per)])
            for i in range(per):
                x_ref[per * b + i, :, u * LANES : (u + 1) * LANES] = v[i]


def weight_kernel(x_ref, inv_ref, fwd_ref, out_ref):
    src, rows, slots = x_ref.shape
    high = lax.Precision.HIGHEST
    x = x_ref[...].reshape(src * rows, slots)
    score = jnp.dot(inv_ref[...], x, precision=high, preferred_element_type=F32)

    def over_slots(row, op):
        row = op(row[:, :LANES], row[:, LANES:])
        row = op(row, pltpu.roll(row, 64, 1))
        row = op(row, pltpu.roll(row, 32, 1))
        return jnp.concatenate([row, row], axis=1)

    top = jnp.broadcast_to(jnp.max(score, axis=0, keepdims=True), (8, slots))
    top = over_slots(top, jnp.maximum)[0:1]
    grown = jnp.exp(score - top)
    part = jnp.broadcast_to(jnp.sum(grown, axis=0, keepdims=True), (8, slots))
    inverse = 1.0 / over_slots(part, jnp.add)
    weight = grown * inverse[0:1]
    spectrum = jnp.dot(
        fwd_ref[...], weight, precision=lax.Precision.HIGH, preferred_element_type=F32
    )
    out_ref[...] = spectrum.reshape(src, rows, slots).astype(out_ref.dtype)


def sum_kernel(w_ref, cp_ref, cq_ref, hot_ref, c_ref, out_ref, w_s, t_s, sum_s, norm_s):
    src = w_ref.shape[0]
    feats, total = cp_ref.shape
    chunks, classes, wide = hot_ref.shape
    wide = wide // 8
    cyc = feats // 8
    n = total // src
    per = LANES // n
    for b in range(src // per):
        lanes = slice(b * LANES, (b + 1) * LANES)
        for u in range(8 // per):
            v = lane_swap(
                [w_ref[per * b + i, :, u * LANES : (u + 1) * LANES].astype(F32) for i in range(per)]
            )
            for j in range(per):
                w_s[per * u + j, :, lanes] = v[j]

    low = lax.broadcasted_iota(jnp.int32, (8, wide), 0) < 4
    own = classes // src
    per = LANES // own
    doms = cyc // per
    halves = sum_s.shape[0]
    span = feats // halves
    some = cyc // halves
    for h in range(halves):
        rows = slice(h * span, (h + 1) * span)
        for t in range(chunks):
            cols = slice(t * wide, (t + 1) * wide)
            buf = t % 2
            for j in range(8):
                w = w_s[j, :, cols]
                turned = flip_rows(w)
                wc = jnp.where(low, w, turned)
                ws = jnp.where(low, turned, w)
                p = cp_ref[rows, cols].reshape(some, 8, wide)
                q = cq_ref[rows, cols].reshape(some, 8, wide)
                term = p * wc[None] - q * ws[None]
                slot = slice(j * wide, (j + 1) * wide)
                t_s[h, buf, 0:span, slot] = term.reshape(span, wide).astype(BF16)
                c = c_ref[h * some : (h + 1) * some, cols]
                t_s[h, buf, span:, slot] = (c * c * w[0:1]).astype(BF16)
            part = lax.dot_general(t_s[h, buf], hot_ref[t], NT, preferred_element_type=F32)
            if t == 0:
                sum_s[h] = part
            else:
                sum_s[h] += part
        norms = []
        for b in range(classes // LANES):
            norm_s[h, b] = sum_s[h, span:, b * LANES : (b + 1) * LANES]
            rows_q = [norm_s[h, b, pl.ds(q, doms // halves, stride=per), :] for q in range(per)]
            norms.append(lane_swap(rows_q))
        for d in range(doms // halves):
            for b in range(classes // LANES):
                lanes = slice(b * LANES, (b + 1) * LANES)
                v = [sum_s[h, 8 * (d * per + q) : 8 * (d * per + q) + 8, lanes] for q in range(per)]
                v = lane_swap(v)
                for k in range(per):
                    part = v[k].astype(BF16)
                    to = (h * doms // halves + d) * src + per * b + k
                    for g in range(4):
                        out_ref[to, :, g * LANES : (g + 1) * LANES] = part[2 * g : 2 * g + 2]
                    norm = jnp.broadcast_to(norms[b][k][d : d + 1], (2, LANES))
                    out_ref[to, :, 4 * LANES :] = norm.astype(BF16)


def finish_kernel(in_ref, order_ref, out_ref, out_s):
    own, part, width = out_ref.shape
    every = in_ref.shape[0]
    src = width // 8
    x = jnp.zeros((width, LANES), F32)
    for g in range(4):
        rows = in_ref[:, :, g * LANES : (g + 1) * LANES].reshape(2 * every, LANES)
        x += jnp.dot(order_ref[g], rows, preferred_element_type=F32)
    norm = in_ref[0, :, 4 * LANES :].astype(F32)
    for d in range(1, every // src):
        norm += in_ref[d * src, :, 4 * LANES :].astype(F32)
    x = jnp.concatenate([x, jnp.broadcast_to(norm[0:1], (8, LANES))], axis=0)
    x = x.T
    x = x[:, :width] / (x[:, width : width + 1] + 1.0)
    for q in range(part):
        for k in range(width // LANES):
            lanes = slice(k * LANES, (k + 1) * LANES)
            out_s[k, pl.ds(q, own, stride=part), :] = x[q * own : (q + 1) * own, lanes]
    for k in range(width // LANES):
        out_ref[:, :, k * LANES : (k + 1) * LANES] = out_s[k].reshape(own, part, LANES)


def call(kernel, shapes, scratch, *args, space=pltpu.VMEM, limit=24):
    many = isinstance(shapes, (list, tuple)) and not hasattr(shapes, "dtype")
    spec = pl.BlockSpec(memory_space=pltpu.VMEM)
    return pl.pallas_call(
        kernel,
        out_shape=shapes,
        in_specs=[pl.BlockSpec(memory_space=space)] * len(args),
        out_specs=[spec] * len(shapes) if many else spec,
        scratch_shapes=scratch,
        compiler_params=pltpu.CompilerParams(vmem_limit_bytes=limit << 20),
    )(*args)


def on_device(images, references, ctf_table, defocus, priors):
    owners = lax.axis_size("cls")
    doms = lax.axis_size("dom")
    n, cyc, ang = images.shape
    own = references.shape[0]
    total = owners * n
    classes = owners * own
    feats = 8 * cyc
    wide = 256
    forward, inverse, order = tables(ang, owners)
    pairs = order.reshape(owners, 4, 2, ang).transpose(1, 3, 0, 2).reshape(4, ang, 2 * owners)
    pairs = np.tile(pairs, (1, 1, doms))
    shape = jax.ShapeDtypeStruct
    pri = priors.T
    group = defocus.reshape(1, n)

    def exchange(x, axis):
        return lax.all_to_all(x, axis, split_axis=0, concat_axis=0, tiled=True)

    rows = 8 * (cyc * (n + own) // LANES + 1)
    sent = call(
        harmonics_kernel,
        shape((owners, rows, LANES), BF16),
        [
            pltpu.VMEM((n, cyc, ang), BF16),
            pltpu.VMEM((own, cyc, ang), BF16),
            pltpu.VMEM((8, n), jnp.int32),
            pltpu.VMEM((1, n), jnp.int32),
            pltpu.VMEM((ang, ang), BF16),
            pltpu.VMEM((ang // LANES, n * cyc, LANES), F32),
            pltpu.VMEM((ang // LANES, own * cyc, LANES), F32),
            pltpu.VMEM((8, LANES), F32),
            pltpu.SemaphoreType.DMA((5,)),
        ],
        *[pltpu.with_memory_space_constraint(x, pltpu.HBM) for x in (images, references, pri, group)],
        pltpu.with_memory_space_constraint(jnp.asarray(forward, BF16), pltpu.HBM),
        space=pltpu.HBM,
    )
    got = exchange(sent, "cls")
    x, cp, cq, hot, ctf = call(
        lambda *refs: score_kernel(own, *refs),
        [
            shape((owners, 8, 8 * n), F32),
            shape((feats, total), F32),
            shape((feats, total), F32),
            shape((total // wide, classes, 8 * wide), BF16),
            shape((cyc, total), F32),
        ],
        [
            pltpu.VMEM((8, total), jnp.int32),
            pltpu.VMEM((feats, classes), BF16),
            pltpu.VMEM((8, 8, total), F32),
        ],
        got,
        ctf_table,
        swap_table(LANES // n),
        swap_table(LANES // own),
    )
    x = exchange(x, "cls")
    spectrum = call(
        weight_kernel,
        shape((owners, 8, 8 * n), BF16),
        [],
        x,
        jnp.asarray(inverse),
        jnp.asarray(forward),
    )
    spectrum = exchange(spectrum, "cls")
    sums = call(
        sum_kernel,
        shape((doms * owners, 2, 5 * LANES), BF16),
        [
            pltpu.VMEM((8, 8, total), F32),
            pltpu.VMEM((2, 2, (feats + cyc) // 2, 8 * wide), BF16),
            pltpu.VMEM((2, (feats + cyc) // 2, classes), F32),
            pltpu.VMEM((2, classes // LANES, cyc // 2, LANES), F32),
        ],
        spectrum,
        cp,
        cq,
        hot,
        ctf,
    )
    sums = exchange(sums, ("dom", "cls"))
    return call(
        finish_kernel,
        shape((own, cyc // doms, ang), F32),
        [pltpu.VMEM((ang // LANES, own * cyc // doms, LANES), F32)],
        sums,
        jnp.asarray(pairs, BF16),
    )


def solution(mesh):
    return jax.shard_map(
        on_device,
        mesh=mesh,
        in_specs=(
            P(("dom", "cls"), None, None),
            P("cls", None, None),
            P(),
            P(("dom", "cls")),
            P(("dom", "cls"), None),
        ),
        out_specs=P("cls", "dom", None),
        check_vma=False,
    )
```

```python
import numpy as np

import jax
import jax.numpy as jnp
from jax import lax
from jax.experimental import pallas as pl
from jax.experimental.pallas import tpu as pltpu
from jax.sharding import PartitionSpec as P

F32 = jnp.float32
BF16 = jnp.bfloat16
NT = (((1,), (1,)), ((), ()))
LANES = 128


def tables(angles, slices):
    harm = angles // 2
    per = harm // slices
    s, c, m = np.meshgrid(np.arange(slices), np.arange(2), np.arange(per), indexing="ij")
    harmonic = (s * per + m).reshape(-1)
    is_sin = c.reshape(-1)
    phase = (harmonic[:, None] * np.arange(angles)[None, :]) % angles
    grid = phase * (2.0 * np.pi / angles)
    cosine = np.cos(grid).astype(np.float32)
    sine = np.sin(grid).astype(np.float32)
    forward = np.where(is_sin[:, None] == 0, cosine, sine).astype(np.float32)
    weight = np.where(harmonic == 0, 1.0, 2.0).astype(np.float32) / angles
    inverse = (np.where(is_sin[:, None] == 0, cosine, -sine) * weight[:, None]).T.astype(np.float32)
    column = is_sin * harm + harmonic
    order = np.zeros((angles, angles), np.float32)
    order[np.arange(angles), column] = 1.0
    return forward, inverse, order


def swap_table(count):
    size = count * LANES
    to = np.arange(size).reshape(count, count, LANES // count).transpose(1, 0, 2).reshape(-1)
    table = np.zeros((size, size), np.float32)
    table[to, np.arange(size)] = 1.0
    return jnp.asarray(table, BF16)


def lane_swap(arrays):
    n = len(arrays)
    width = LANES // n
    arrays = list(arrays)
    lane = lax.broadcasted_iota(jnp.int32, arrays[0].shape, 1)
    step = n // 2
    while step >= 1:
        shift = width * step
        low = (lane & shift) == 0
        for a in range(n):
            if a & step == 0:
                x, y = arrays[a], arrays[a + step]
                arrays[a] = jnp.where(low, x, pltpu.roll(y, shift, 1))
                arrays[a + step] = jnp.where(low, pltpu.roll(x, LANES - shift, 1), y)
        step //= 2
    return arrays


def harmonics_kernel(img_hbm, ref_hbm, pri_hbm, def_hbm, fwd_hbm, out_ref, *scratch):
    img_ref, ref_ref, pri_ref, def_ref, fwd_ref, img_s, ref_s, int_s, sems = scratch
    n, cyc, ang = img_ref.shape
    own = ref_ref.shape[0]
    dest = out_ref.shape[0]
    rows_p = 8 * cyc * n // LANES
    rows_r = 8 * cyc * own // LANES
    pairs = (
        (fwd_hbm, fwd_ref),
        (ref_hbm, ref_ref),
        (img_hbm, img_ref),
        (pri_hbm, pri_ref),
        (def_hbm, def_ref),
    )
    copies = [pltpu.make_async_copy(a, b, sems.at[k]) for k, (a, b) in enumerate(pairs)]
    for copy in copies:
        copy.start()

    def part(ref, src, count, start):
        for k in range(ang // LANES):
            src[k] = ref[:, :, k * LANES : (k + 1) * LANES].astype(F32).reshape(count * cyc, LANES)
        wide = 2 * LANES
        group = wide // count
        for c in range(cyc // group):
            block = jnp.concatenate(
                [
                    jnp.concatenate(
                        [src[k, pl.ds(group * c + q, count, stride=cyc), :] for q in range(group)],
                        axis=0,
                    )
                    for k in range(ang // LANES)
                ],
                axis=1,
            ).astype(BF16)
            y = lax.dot_general(fwd_ref[...], block, NT, preferred_element_type=F32)
            y = y.reshape(dest, 8, wide)
            y = jnp.concatenate([y[:, :, :LANES], y[:, :, LANES:]], axis=1)
            out_ref[:, start + 16 * c : start + 16 * (c + 1), :] = y.astype(BF16)

    copies[0].wait()
    copies[1].wait()
    part(ref_ref, ref_s, own, rows_p)
    copies[2].wait()
    part(img_ref, img_s, n, 0)
    copies[3].wait()
    copies[4].wait()
    int_s[...] = jnp.zeros_like(int_s)
    int_s[:, 0:n] = (pri_ref[...] - dest * own // 2).astype(F32)
    int_s[0:1, n : 2 * n] = def_ref[...].astype(F32)
    out_ref[:, (rows_p + rows_r) :, :] = jnp.broadcast_to(
        int_s[...].astype(BF16)[None], (dest, 8, LANES)
    )


def one_hot(row, count):
    wide = row.shape[1]
    index = lax.broadcasted_iota(jnp.int32, (count, wide), 0).astype(jnp.int16)
    row = jnp.broadcast_to(row, (16, wide)).astype(jnp.int16)
    hot = index.reshape(count // 16, 16, wide) == row[None]
    return jnp.where(hot, jnp.ones((), BF16), jnp.zeros((), BF16)).reshape(count, wide)


def flip_rows(x):
    return pltpu.roll(x, 4, x.ndim - 2)


def score_kernel(own, in_ref, ctf_ref, swap_p_ref, swap_r_ref, x_ref, cp_ref, cq_ref, hot_ref, c_ref, cid_s, rt_s, x_s):
    src = in_ref.shape[0]
    groups, cyc = ctf_ref.shape
    total = cp_ref.shape[1]
    n = total // src
    rows_p = 8 * cyc * n // LANES
    rows_r = 8 * cyc * own // LANES
    per = LANES // n
    per_r = LANES // own
    blocks = src // per

    ctf = ctf_ref[...]
    parts = []
    for _ in range(3):
        parts.append(ctf.astype(BF16).astype(F32))
        ctf = ctf - parts[-1]
    parts = jnp.concatenate(parts, axis=0).T.astype(BF16)
    hots = []
    for b in range(blocks):
        lanes = slice(b * LANES, (b + 1) * LANES)
        v = lane_swap(
            [in_ref[per * b + i, (rows_p + rows_r) :, :].astype(F32) for i in range(per)]
        )
        cid_s[:, lanes] = v[0].astype(jnp.int32) + src * own // 2
        group = v[1][0:1].astype(jnp.int32)
        hots.append((lax.broadcasted_iota(jnp.int32, (groups, LANES), 0) == group).astype(F32))
    hots = jnp.concatenate(hots, axis=1)
    hots = jnp.concatenate([hots] * 3, axis=0).astype(BF16)
    c_ref[...] = jnp.dot(parts, hots, preferred_element_type=F32)

    def swapped(sources, first, last, size, table):
        blocks = [
            jnp.concatenate([in_ref[b + i, first:last, :] for i in range(size)], axis=1)
            for b in range(sources.start, sources.stop, size)
        ]
        return jnp.dot(jnp.concatenate(blocks, axis=0), table[...], preferred_element_type=F32)

    every = swapped(range(src), rows_p, rows_p + rows_r, per_r, swap_r_ref).astype(BF16)
    for b in range(src // per_r):
        y = every[b * rows_r : (b + 1) * rows_r].reshape(rows_r // 8, 8, per_r * LANES)
        for c in range(rows_r // 8):
            for q in range(0, per_r, 2):
                pair = [y[c, :, (q + k) * LANES : (q + k + 1) * LANES] for k in range(2)]
                row = (per_r * c + q) * 8
                rt_s[row : row + 16, b * LANES : (b + 1) * LANES] = jnp.concatenate(pair, axis=0)

    upper = lax.broadcasted_iota(jnp.int32, (8, LANES), 0) >= 4

    def scale(b, y):
        lanes = slice(b * LANES, (b + 1) * LANES)
        ctf = c_ref[:, lanes]
        for c in range(rows_p // 8):
            for q in range(per):
                r = per * c + q
                p = y[8 * c : 8 * c + 8, q * LANES : (q + 1) * LANES]
                p = p * jnp.broadcast_to(ctf[r : r + 1], (8, LANES))
                cp_ref[8 * r : 8 * r + 8, lanes] = p
                turned = flip_rows(p)
                cq_ref[8 * r : 8 * r + 8, lanes] = jnp.where(upper, turned, -turned)

    chunks, classes, wide = hot_ref.shape
    wide = wide // 8
    low = lax.broadcasted_iota(jnp.int32, (8, wide), 0) < 4

    for t in range(chunks):
        cols = slice(t * wide, (t + 1) * wide)
        if t % 2 == 0:
            sources = range(t * wide // n, (t + 2) * wide // n)
            every = swapped(sources, 0, rows_p, per, swap_p_ref)
        for b in range(wide // LANES):
            at = (t % 2 * wide // LANES + b) * rows_p
            scale(t * wide // LANES + b, every[at : at + rows_p])
        for j in range(8):
            hot = one_hot(cid_s[j : j + 1, cols], classes)
            hot_ref[t, :, j * wide : (j + 1) * wide] = hot
            picked = jnp.dot(rt_s[...], hot, preferred_element_type=F32)
            re = jnp.sum((cp_ref[:, cols] * picked).reshape(cyc, 8, wide), axis=0)
            im = jnp.sum((cq_ref[:, cols] * picked).reshape(cyc, 8, wide), axis=0)
            x_s[j, :, cols] = jnp.where(low, re + flip_rows(re), im + flip_rows(im))

    for b in range(blocks):
        lanes = slice(b * LANES, (b + 1) * LANES)
        for u in range(8 // per):
            v = lane_swap([x_s[per * u + j, :, lanes] for j in range(per)])
            for i in range(per):
                x_ref[per * b + i, :, u * LANES : (u + 1) * LANES] = v[i]


def weight_kernel(x_ref, inv_ref, fwd_ref, out_ref):
    src, rows, slots = x_ref.shape
    high = lax.Precision.HIGHEST
    x = x_ref[...].reshape(src * rows, slots)
    score = jnp.dot(inv_ref[...], x, precision=high, preferred_element_type=F32)

    def over_slots(row, op):
        row = op(row[:, :LANES], row[:, LANES:])
        row = op(row, pltpu.roll(row, 64, 1))
        row = op(row, pltpu.roll(row, 32, 1))
        return jnp.concatenate([row, row], axis=1)

    top = jnp.broadcast_to(jnp.max(score, axis=0, keepdims=True), (8, slots))
    top = over_slots(top, jnp.maximum)[0:1]
    grown = jnp.exp(score - top)
    part = jnp.broadcast_to(jnp.sum(grown, axis=0, keepdims=True), (8, slots))
    inverse = 1.0 / over_slots(part, jnp.add)
    weight = grown * inverse[0:1]
    spectrum = jnp.dot(
        fwd_ref[...], weight, precision=lax.Precision.HIGH, preferred_element_type=F32
    )
    out_ref[...] = spectrum.reshape(src, rows, slots).astype(out_ref.dtype)


def sum_kernel(w_ref, cp_ref, cq_ref, hot_ref, c_ref, out_ref, w_s, t_s, sum_s, norm_s):
    src = w_ref.shape[0]
    feats, total = cp_ref.shape
    chunks, classes, wide = hot_ref.shape
    wide = wide // 8
    cyc = feats // 8
    n = total // src
    per = LANES // n
    for b in range(src // per):
        lanes = slice(b * LANES, (b + 1) * LANES)
        for u in range(8 // per):
            v = lane_swap(
                [w_ref[per * b + i, :, u * LANES : (u + 1) * LANES].astype(F32) for i in range(per)]
            )
            for j in range(per):
                w_s[per * u + j, :, lanes] = v[j]

    low = lax.broadcasted_iota(jnp.int32, (8, wide), 0) < 4
    own = classes // src
    per = LANES // own
    doms = cyc // per
    halves = sum_s.shape[0]
    span = feats // halves
    some = cyc // halves
    for h in range(halves):
        rows = slice(h * span, (h + 1) * span)
        for t in range(chunks):
            cols = slice(t * wide, (t + 1) * wide)
            buf = t % 2
            for j in range(8):
                w = w_s[j, :, cols]
                turned = flip_rows(w)
                wc = jnp.where(low, w, turned)
                ws = jnp.where(low, turned, w)
                p = cp_ref[rows, cols].reshape(some, 8, wide)
                q = cq_ref[rows, cols].reshape(some, 8, wide)
                term = p * wc[None] - q * ws[None]
                slot = slice(j * wide, (j + 1) * wide)
                t_s[h, buf, 0:span, slot] = term.reshape(span, wide).astype(BF16)
                c = c_ref[h * some : (h + 1) * some, cols]
                t_s[h, buf, span:, slot] = (c * c * w[0:1]).astype(BF16)
            part = lax.dot_general(t_s[h, buf], hot_ref[t], NT, preferred_element_type=F32)
            if t == 0:
                sum_s[h] = part
            else:
                sum_s[h] += part
        norms = []
        for b in range(classes // LANES):
            norm_s[h, b] = sum_s[h, span:, b * LANES : (b + 1) * LANES]
            rows_q = [norm_s[h, b, pl.ds(q, doms // halves, stride=per), :] for q in range(per)]
            norms.append(lane_swap(rows_q))
        for d in range(doms // halves):
            for b in range(classes // LANES):
                lanes = slice(b * LANES, (b + 1) * LANES)
                v = [sum_s[h, 8 * (d * per + q) : 8 * (d * per + q) + 8, lanes] for q in range(per)]
                v = lane_swap(v)
                for k in range(per):
                    part = v[k].astype(BF16)
                    to = (h * doms // halves + d) * src + per * b + k
                    for g in range(4):
                        out_ref[to, :, g * LANES : (g + 1) * LANES] = part[2 * g : 2 * g + 2]
                    norm = jnp.broadcast_to(norms[b][k][d : d + 1], (2, LANES))
                    out_ref[to, :, 4 * LANES :] = norm.astype(BF16)


def finish_kernel(in_ref, order_ref, out_ref, out_s):
    own, part, width = out_ref.shape
    every = in_ref.shape[0]
    src = width // 8
    x = jnp.zeros((width, LANES), F32)
    for g in range(4):
        rows = in_ref[:, :, g * LANES : (g + 1) * LANES].reshape(2 * every, LANES)
        x += jnp.dot(order_ref[g], rows, preferred_element_type=F32)
    norm = in_ref[0, :, 4 * LANES :].astype(F32)
    for d in range(1, every // src):
        norm += in_ref[d * src, :, 4 * LANES :].astype(F32)
    x = jnp.concatenate([x, jnp.broadcast_to(norm[0:1], (8, LANES))], axis=0)
    x = x.T
    x = x[:, :width] / (x[:, width : width + 1] + 1.0)
    for q in range(part):
        for k in range(width // LANES):
            lanes = slice(k * LANES, (k + 1) * LANES)
            out_s[k, pl.ds(q, own, stride=part), :] = x[q * own : (q + 1) * own, lanes]
    for k in range(width // LANES):
        out_ref[:, :, k * LANES : (k + 1) * LANES] = out_s[k].reshape(own, part, LANES)


def call(kernel, shapes, scratch, *args, space=pltpu.VMEM, limit=24):
    many = isinstance(shapes, (list, tuple)) and not hasattr(shapes, "dtype")
    spec = pl.BlockSpec(memory_space=pltpu.VMEM)
    return pl.pallas_call(
        kernel,
        out_shape=shapes,
        in_specs=[pl.BlockSpec(memory_space=space)] * len(args),
        out_specs=[spec] * len(shapes) if many else spec,
        scratch_shapes=scratch,
        compiler_params=pltpu.CompilerParams(vmem_limit_bytes=limit << 20),
    )(*args)


def on_device(images, references, ctf_table, defocus, priors):
    owners = lax.axis_size("cls")
    doms = lax.axis_size("dom")
    n, cyc, ang = images.shape
    own = references.shape[0]
    total = owners * n
    classes = owners * own
    feats = 8 * cyc
    wide = 256
    forward, inverse, order = tables(ang, owners)
    pairs = order.reshape(owners, 4, 2, ang).transpose(1, 3, 0, 2).reshape(4, ang, 2 * owners)
    pairs = np.tile(pairs, (1, 1, doms))
    shape = jax.ShapeDtypeStruct
    pri = priors.T
    group = defocus.reshape(1, n)

    def exchange(x, axis):
        return lax.all_to_all(x, axis, split_axis=0, concat_axis=0, tiled=True)

    rows = 8 * (cyc * (n + own) // LANES + 1)
    sent = call(
        harmonics_kernel,
        shape((owners, rows, LANES), BF16),
        [
            pltpu.VMEM((n, cyc, ang), BF16),
            pltpu.VMEM((own, cyc, ang), BF16),
            pltpu.VMEM((8, n), jnp.int32),
            pltpu.VMEM((1, n), jnp.int32),
            pltpu.VMEM((ang, ang), BF16),
            pltpu.VMEM((ang // LANES, n * cyc, LANES), F32),
            pltpu.VMEM((ang // LANES, own * cyc, LANES), F32),
            pltpu.VMEM((8, LANES), F32),
            pltpu.SemaphoreType.DMA((5,)),
        ],
        *[pltpu.with_memory_space_constraint(x, pltpu.HBM) for x in (images, references, pri, group)],
        pltpu.with_memory_space_constraint(jnp.asarray(forward, BF16), pltpu.HBM),
        space=pltpu.HBM,
    )
    got = exchange(sent, "cls")
    x, cp, cq, hot, ctf = call(
        lambda *refs: score_kernel(own, *refs),
        [
            shape((owners, 8, 8 * n), F32),
            shape((feats, total), F32),
            shape((feats, total), F32),
            shape((total // wide, classes, 8 * wide), BF16),
            shape((cyc, total), F32),
        ],
        [
            pltpu.VMEM((8, total), jnp.int32),
            pltpu.VMEM((feats, classes), BF16),
            pltpu.VMEM((8, 8, total), F32),
        ],
        got,
        ctf_table,
        swap_table(LANES // n),
        swap_table(LANES // own),
    )
    x = exchange(x, "cls")
    spectrum = call(
        weight_kernel,
        shape((owners, 8, 8 * n), BF16),
        [],
        x,
        jnp.asarray(inverse),
        jnp.asarray(forward),
    )
    spectrum = exchange(spectrum, "cls")
    sums = call(
        sum_kernel,
        shape((doms * owners, 2, 5 * LANES), BF16),
        [
            pltpu.VMEM((8, 8, total), F32),
            pltpu.VMEM((2, 2, (feats + cyc) // 2, 8 * wide), BF16),
            pltpu.VMEM((2, (feats + cyc) // 2, classes), F32),
            pltpu.VMEM((2, classes // LANES, cyc // 2, LANES), F32),
        ],
        spectrum,
        cp,
        cq,
        hot,
        ctf,
    )
    sums = exchange(sums, ("dom", "cls"))
    return call(
        finish_kernel,
        shape((own, cyc // doms, ang), F32),
        [pltpu.VMEM((ang // LANES, own * cyc // doms, LANES), F32)],
        sums,
        jnp.asarray(pairs, BF16),
    )


def solution(mesh):
    return jax.shard_map(
        on_device,
        mesh=mesh,
        in_specs=(
            P(("dom", "cls"), None, None),
            P("cls", None, None),
            P(),
            P(("dom", "cls")),
            P(("dom", "cls"), None),
        ),
        out_specs=P("cls", "dom", None),
        check_vma=False,
    )
```

```python
import numpy as np

import jax
import jax.numpy as jnp
from jax import lax
from jax.experimental import pallas as pl
from jax.experimental.pallas import tpu as pltpu
from jax.sharding import PartitionSpec as P

F32 = jnp.float32
BF16 = jnp.bfloat16
NT = (((1,), (1,)), ((), ()))
LANES = 128


def tables(angles, slices):
    harm = angles // 2
    per = harm // slices
    s, c, m = np.meshgrid(np.arange(slices), np.arange(2), np.arange(per), indexing="ij")
    harmonic = (s * per + m).reshape(-1)
    is_sin = c.reshape(-1)
    phase = (harmonic[:, None] * np.arange(angles)[None, :]) % angles
    grid = phase * (2.0 * np.pi / angles)
    cosine = np.cos(grid).astype(np.float32)
    sine = np.sin(grid).astype(np.float32)
    forward = np.where(is_sin[:, None] == 0, cosine, sine).astype(np.float32)
    weight = np.where(harmonic == 0, 1.0, 2.0).astype(np.float32) / angles
    inverse = (np.where(is_sin[:, None] == 0, cosine, -sine) * weight[:, None]).T.astype(np.float32)
    column = is_sin * harm + harmonic
    order = np.zeros((angles, angles), np.float32)
    order[np.arange(angles), column] = 1.0
    return forward, inverse, order


def swap_table(count):
    size = count * LANES
    to = np.arange(size).reshape(count, count, LANES // count).transpose(1, 0, 2).reshape(-1)
    table = np.zeros((size, size), np.float32)
    table[to, np.arange(size)] = 1.0
    return jnp.asarray(table, BF16)


def lane_swap(arrays):
    n = len(arrays)
    width = LANES // n
    arrays = list(arrays)
    lane = lax.broadcasted_iota(jnp.int32, arrays[0].shape, 1)
    step = n // 2
    while step >= 1:
        shift = width * step
        low = (lane & shift) == 0
        for a in range(n):
            if a & step == 0:
                x, y = arrays[a], arrays[a + step]
                arrays[a] = jnp.where(low, x, pltpu.roll(y, shift, 1))
                arrays[a + step] = jnp.where(low, pltpu.roll(x, LANES - shift, 1), y)
        step //= 2
    return arrays


def harmonics_kernel(img_hbm, ref_hbm, pri_hbm, def_hbm, fwd_hbm, out_ref, *scratch):
    img_ref, ref_ref, pri_ref, def_ref, fwd_ref, img_s, ref_s, int_s, sems = scratch
    n, cyc, ang = img_ref.shape
    own = ref_ref.shape[0]
    dest = out_ref.shape[0]
    rows_p = 8 * cyc * n // LANES
    rows_r = 8 * cyc * own // LANES
    pairs = (
        (fwd_hbm, fwd_ref),
        (ref_hbm, ref_ref),
        (img_hbm.at[0 : n // 2], img_ref.at[0 : n // 2]),
        (pri_hbm, pri_ref),
        (def_hbm, def_ref),
        (img_hbm.at[n // 2 : n], img_ref.at[n // 2 : n]),
    )
    copies = [pltpu.make_async_copy(a, b, sems.at[k]) for k, (a, b) in enumerate(pairs)]
    for copy in copies:
        copy.start()

    def part(ref, src, count, start):
        for k in range(ang // LANES):
            src[k] = ref[:, :, k * LANES : (k + 1) * LANES].astype(F32).reshape(count * cyc, LANES)
        wide = 2 * LANES
        group = wide // count
        for c in range(cyc // group):
            block = jnp.concatenate(
                [
                    jnp.concatenate(
                        [src[k, pl.ds(group * c + q, count, stride=cyc), :] for q in range(group)],
                        axis=0,
                    )
                    for k in range(ang // LANES)
                ],
                axis=1,
            ).astype(BF16)
            y = lax.dot_general(fwd_ref[...], block, NT, preferred_element_type=F32)
            y = y.reshape(dest, 8, wide)
            y = jnp.concatenate([y[:, :, :LANES], y[:, :, LANES:]], axis=1)
            out_ref[:, start + 16 * c : start + 16 * (c + 1), :] = y.astype(BF16)

    copies[0].wait()
    copies[1].wait()
    part(ref_ref, ref_s, own, rows_p)
    copies[2].wait()
    copies[5].wait()
    part(img_ref, img_s, n, 0)
    copies[3].wait()
    copies[4].wait()
    int_s[...] = jnp.zeros_like(int_s)
    int_s[:, 0:n] = (pri_ref[...] - dest * own // 2).astype(F32)
    int_s[0:1, n : 2 * n] = def_ref[...].astype(F32)
    out_ref[:, (rows_p + rows_r) :, :] = jnp.broadcast_to(
        int_s[...].astype(BF16)[None], (dest, 8, LANES)
    )


def one_hot(row, count):
    wide = row.shape[1]
    index = lax.broadcasted_iota(jnp.int32, (count, wide), 0).astype(jnp.int16)
    row = jnp.broadcast_to(row, (16, wide)).astype(jnp.int16)
    hot = index.reshape(count // 16, 16, wide) == row[None]
    return jnp.where(hot, jnp.ones((), BF16), jnp.zeros((), BF16)).reshape(count, wide)


def flip_rows(x):
    return pltpu.roll(x, 4, x.ndim - 2)


def score_kernel(own, in_ref, ctf_ref, swap_p_ref, swap_r_ref, x_ref, cp_ref, cq_ref, hot_ref, c_ref, cid_s, rt_s, x_s):
    src = in_ref.shape[0]
    groups, cyc = ctf_ref.shape
    total = cp_ref.shape[1]
    n = total // src
    rows_p = 8 * cyc * n // LANES
    rows_r = 8 * cyc * own // LANES
    per = LANES // n
    per_r = LANES // own
    blocks = src // per

    ctf = ctf_ref[...]
    parts = []
    for _ in range(3):
        parts.append(ctf.astype(BF16).astype(F32))
        ctf = ctf - parts[-1]
    parts = jnp.concatenate(parts, axis=0).T.astype(BF16)
    hots = []
    for b in range(blocks):
        lanes = slice(b * LANES, (b + 1) * LANES)
        v = lane_swap(
            [in_ref[per * b + i, (rows_p + rows_r) :, :].astype(F32) for i in range(per)]
        )
        cid_s[:, lanes] = v[0].astype(jnp.int32) + src * own // 2
        group = v[1][0:1].astype(jnp.int32)
        hots.append((lax.broadcasted_iota(jnp.int32, (groups, LANES), 0) == group).astype(F32))
    hots = jnp.concatenate(hots, axis=1)
    hots = jnp.concatenate([hots] * 3, axis=0).astype(BF16)
    c_ref[...] = jnp.dot(parts, hots, preferred_element_type=F32)

    def swapped(sources, first, last, size, table):
        blocks = [
            jnp.concatenate([in_ref[b + i, first:last, :] for i in range(size)], axis=1)
            for b in range(sources.start, sources.stop, size)
        ]
        return jnp.dot(jnp.concatenate(blocks, axis=0), table[...], preferred_element_type=F32)

    every = swapped(range(src), rows_p, rows_p + rows_r, per_r, swap_r_ref).astype(BF16)
    for b in range(src // per_r):
        y = every[b * rows_r : (b + 1) * rows_r].reshape(rows_r // 8, 8, per_r * LANES)
        for c in range(rows_r // 8):
            for q in range(0, per_r, 2):
                pair = [y[c, :, (q + k) * LANES : (q + k + 1) * LANES] for k in range(2)]
                row = (per_r * c + q) * 8
                rt_s[row : row + 16, b * LANES : (b + 1) * LANES] = jnp.concatenate(pair, axis=0)

    upper = lax.broadcasted_iota(jnp.int32, (8, LANES), 0) >= 4

    def scale(b, y):
        lanes = slice(b * LANES, (b + 1) * LANES)
        ctf = c_ref[:, lanes]
        for c in range(rows_p // 8):
            for q in range(per):
                r = per * c + q
                p = y[8 * c : 8 * c + 8, q * LANES : (q + 1) * LANES]
                p = p * jnp.broadcast_to(ctf[r : r + 1], (8, LANES))
                cp_ref[8 * r : 8 * r + 8, lanes] = p
                turned = flip_rows(p)
                cq_ref[8 * r : 8 * r + 8, lanes] = jnp.where(upper, turned, -turned)

    chunks, classes, wide = hot_ref.shape
    wide = wide // 8
    low = lax.broadcasted_iota(jnp.int32, (8, wide), 0) < 4

    for t in range(chunks):
        cols = slice(t * wide, (t + 1) * wide)
        if t % 2 == 0:
            sources = range(t * wide // n, (t + 2) * wide // n)
            every = swapped(sources, 0, rows_p, per, swap_p_ref)
        for b in range(wide // LANES):
            at = (t % 2 * wide // LANES + b) * rows_p
            scale(t * wide // LANES + b, every[at : at + rows_p])
        for j in range(8):
            hot = one_hot(cid_s[j : j + 1, cols], classes)
            hot_ref[t, :, j * wide : (j + 1) * wide] = hot
            picked = jnp.dot(rt_s[...], hot, preferred_element_type=F32)
            re = jnp.sum((cp_ref[:, cols] * picked).reshape(cyc, 8, wide), axis=0)
            im = jnp.sum((cq_ref[:, cols] * picked).reshape(cyc, 8, wide), axis=0)
            x_s[j, :, cols] = jnp.where(low, re + flip_rows(re), im + flip_rows(im))

    for b in range(blocks):
        lanes = slice(b * LANES, (b + 1) * LANES)
        for u in range(8 // per):
            v = lane_swap([x_s[per * u + j, :, lanes] for j in range(per)])
            for i in range(per):
                x_ref[per * b + i, :, u * LANES : (u + 1) * LANES] = v[i]


def weight_kernel(x_ref, inv_ref, fwd_ref, out_ref):
    src, rows, slots = x_ref.shape
    high = lax.Precision.HIGHEST
    x = x_ref[...].reshape(src * rows, slots)
    score = jnp.dot(inv_ref[...], x, precision=high, preferred_element_type=F32)

    def over_slots(row, op):
        row = op(row[:, :LANES], row[:, LANES:])
        row = op(row, pltpu.roll(row, 64, 1))
        row = op(row, pltpu.roll(row, 32, 1))
        return jnp.concatenate([row, row], axis=1)

    top = jnp.broadcast_to(jnp.max(score, axis=0, keepdims=True), (8, slots))
    top = over_slots(top, jnp.maximum)[0:1]
    grown = jnp.exp(score - top)
    part = jnp.broadcast_to(jnp.sum(grown, axis=0, keepdims=True), (8, slots))
    inverse = 1.0 / over_slots(part, jnp.add)
    weight = grown * inverse[0:1]
    spectrum = jnp.dot(
        fwd_ref[...], weight, precision=lax.Precision.HIGH, preferred_element_type=F32
    )
    out_ref[...] = spectrum.reshape(src, rows, slots).astype(out_ref.dtype)


def sum_kernel(w_ref, cp_ref, cq_ref, hot_ref, c_ref, out_ref, w_s, t_s, sum_s, norm_s):
    src = w_ref.shape[0]
    feats, total = cp_ref.shape
    chunks, classes, wide = hot_ref.shape
    wide = wide // 8
    cyc = feats // 8
    n = total // src
    per = LANES // n
    for b in range(src // per):
        lanes = slice(b * LANES, (b + 1) * LANES)
        for u in range(8 // per):
            v = lane_swap(
                [w_ref[per * b + i, :, u * LANES : (u + 1) * LANES].astype(F32) for i in range(per)]
            )
            for j in range(per):
                w_s[per * u + j, :, lanes] = v[j]

    low = lax.broadcasted_iota(jnp.int32, (8, wide), 0) < 4
    own = classes // src
    per = LANES // own
    doms = cyc // per
    halves = sum_s.shape[0]
    span = feats // halves
    some = cyc // halves
    for h in range(halves):
        rows = slice(h * span, (h + 1) * span)
        for t in range(chunks):
            cols = slice(t * wide, (t + 1) * wide)
            buf = t % 2
            for j in range(8):
                w = w_s[j, :, cols]
                turned = flip_rows(w)
                wc = jnp.where(low, w, turned)
                ws = jnp.where(low, turned, w)
                p = cp_ref[rows, cols].reshape(some, 8, wide)
                q = cq_ref[rows, cols].reshape(some, 8, wide)
                term = p * wc[None] - q * ws[None]
                slot = slice(j * wide, (j + 1) * wide)
                t_s[h, buf, 0:span, slot] = term.reshape(span, wide).astype(BF16)
                c = c_ref[h * some : (h + 1) * some, cols]
                t_s[h, buf, span:, slot] = (c * c * w[0:1]).astype(BF16)
            part = lax.dot_general(t_s[h, buf], hot_ref[t], NT, preferred_element_type=F32)
            if t == 0:
                sum_s[h] = part
            else:
                sum_s[h] += part
        norms = []
        for b in range(classes // LANES):
            norm_s[h, b] = sum_s[h, span:, b * LANES : (b + 1) * LANES]
            rows_q = [norm_s[h, b, pl.ds(q, doms // halves, stride=per), :] for q in range(per)]
            norms.append(lane_swap(rows_q))
        for d in range(doms // halves):
            for b in range(classes // LANES):
                lanes = slice(b * LANES, (b + 1) * LANES)
                v = [sum_s[h, 8 * (d * per + q) : 8 * (d * per + q) + 8, lanes] for q in range(per)]
                v = lane_swap(v)
                for k in range(per):
                    part = v[k].astype(BF16)
                    to = (h * doms // halves + d) * src + per * b + k
                    for g in range(4):
                        out_ref[to, :, g * LANES : (g + 1) * LANES] = part[2 * g : 2 * g + 2]
                    norm = jnp.broadcast_to(norms[b][k][d : d + 1], (2, LANES))
                    out_ref[to, :, 4 * LANES :] = norm.astype(BF16)


def finish_kernel(in_ref, order_ref, out_ref, out_s):
    own, part, width = out_ref.shape
    every = in_ref.shape[0]
    src = width // 8
    x = jnp.zeros((width, LANES), F32)
    for g in range(4):
        rows = in_ref[:, :, g * LANES : (g + 1) * LANES].reshape(2 * every, LANES)
        x += jnp.dot(order_ref[g], rows, preferred_element_type=F32)
    norm = in_ref[0, :, 4 * LANES :].astype(F32)
    for d in range(1, every // src):
        norm += in_ref[d * src, :, 4 * LANES :].astype(F32)
    x = jnp.concatenate([x, jnp.broadcast_to(norm[0:1], (8, LANES))], axis=0)
    x = x.T
    x = x[:, :width] / (x[:, width : width + 1] + 1.0)
    for q in range(part):
        for k in range(width // LANES):
            lanes = slice(k * LANES, (k + 1) * LANES)
            out_s[k, pl.ds(q, own, stride=part), :] = x[q * own : (q + 1) * own, lanes]
    for k in range(width // LANES):
        out_ref[:, :, k * LANES : (k + 1) * LANES] = out_s[k].reshape(own, part, LANES)


def call(kernel, shapes, scratch, *args, space=pltpu.VMEM, limit=24):
    many = isinstance(shapes, (list, tuple)) and not hasattr(shapes, "dtype")
    spec = pl.BlockSpec(memory_space=pltpu.VMEM)
    return pl.pallas_call(
        kernel,
        out_shape=shapes,
        in_specs=[pl.BlockSpec(memory_space=space)] * len(args),
        out_specs=[spec] * len(shapes) if many else spec,
        scratch_shapes=scratch,
        compiler_params=pltpu.CompilerParams(vmem_limit_bytes=limit << 20),
    )(*args)


def on_device(images, references, ctf_table, defocus, priors):
    owners = lax.axis_size("cls")
    doms = lax.axis_size("dom")
    n, cyc, ang = images.shape
    own = references.shape[0]
    total = owners * n
    classes = owners * own
    feats = 8 * cyc
    wide = 256
    forward, inverse, order = tables(ang, owners)
    pairs = order.reshape(owners, 4, 2, ang).transpose(1, 3, 0, 2).reshape(4, ang, 2 * owners)
    pairs = np.tile(pairs, (1, 1, doms))
    shape = jax.ShapeDtypeStruct
    pri = priors.T
    group = defocus.reshape(1, n)

    def exchange(x, axis):
        return lax.all_to_all(x, axis, split_axis=0, concat_axis=0, tiled=True)

    rows = 8 * (cyc * (n + own) // LANES + 1)
    sent = call(
        harmonics_kernel,
        shape((owners, rows, LANES), BF16),
        [
            pltpu.VMEM((n, cyc, ang), BF16),
            pltpu.VMEM((own, cyc, ang), BF16),
            pltpu.VMEM((8, n), jnp.int32),
            pltpu.VMEM((1, n), jnp.int32),
            pltpu.VMEM((ang, ang), BF16),
            pltpu.VMEM((ang // LANES, n * cyc, LANES), F32),
            pltpu.VMEM((ang // LANES, own * cyc, LANES), F32),
            pltpu.VMEM((8, LANES), F32),
            pltpu.SemaphoreType.DMA((6,)),
        ],
        *[pltpu.with_memory_space_constraint(x, pltpu.HBM) for x in (images, references, pri, group)],
        pltpu.with_memory_space_constraint(jnp.asarray(forward, BF16), pltpu.HBM),
        space=pltpu.HBM,
    )
    got = exchange(sent, "cls")
    x, cp, cq, hot, ctf = call(
        lambda *refs: score_kernel(own, *refs),
        [
            shape((owners, 8, 8 * n), F32),
            shape((feats, total), F32),
            shape((feats, total), F32),
            shape((total // wide, classes, 8 * wide), BF16),
            shape((cyc, total), F32),
        ],
        [
            pltpu.VMEM((8, total), jnp.int32),
            pltpu.VMEM((feats, classes), BF16),
            pltpu.VMEM((8, 8, total), F32),
        ],
        got,
        ctf_table,
        swap_table(LANES // n),
        swap_table(LANES // own),
    )
    x = exchange(x, "cls")
    spectrum = call(
        weight_kernel,
        shape((owners, 8, 8 * n), BF16),
        [],
        x,
        jnp.asarray(inverse),
        jnp.asarray(forward),
    )
    spectrum = exchange(spectrum, "cls")
    sums = call(
        sum_kernel,
        shape((doms * owners, 2, 5 * LANES), BF16),
        [
            pltpu.VMEM((8, 8, total), F32),
            pltpu.VMEM((2, 2, (feats + cyc) // 2, 8 * wide), BF16),
            pltpu.VMEM((2, (feats + cyc) // 2, classes), F32),
            pltpu.VMEM((2, classes // LANES, cyc // 2, LANES), F32),
        ],
        spectrum,
        cp,
        cq,
        hot,
        ctf,
    )
    sums = exchange(sums, ("dom", "cls"))
    return call(
        finish_kernel,
        shape((own, cyc // doms, ang), F32),
        [pltpu.VMEM((ang // LANES, own * cyc // doms, LANES), F32)],
        sums,
        jnp.asarray(pairs, BF16),
    )


def solution(mesh):
    return jax.shard_map(
        on_device,
        mesh=mesh,
        in_specs=(
            P(("dom", "cls"), None, None),
            P("cls", None, None),
            P(),
            P(("dom", "cls")),
            P(("dom", "cls"), None),
        ),
        out_specs=P("cls", "dom", None),
        check_vma=False,
    )
```
